256 devices in a mesh: inp: 32 (over x, z_lo, core), frq: 8 (over y, z_hi).
Axes of the slice: x: 4, y: 4, z: 8 (z_hi: 2, z_lo: 4; z = z_hi * 4 + z_lo), core: 2. Of those that a mesh axis runs over, the one named last changes fastest.
Arguments:
- voltages: bfloat16 [1024, 32, 2048], P('inp', 'frq'), may hold values from -6 to 6
- history: bfloat16 [1024, 3, 2048], P('inp'), may hold values from -6 to 6
- window: float32 [4, 2048], replicated, may hold values from -3 to 3
Outputs:
- visibilities: float32 [1024, 32, 2, 1024], P('frq', 'inp')
The draws below stay inside these ranges and needn't reach their ends.
All inputs are finite; a program needn't handle non-finite values.
Results may differ from the reference program's by a relative error of at most 0.0003.
Values may be sent and summed in bfloat16 or wider, within the bound.
No kernel may reach another device: no remote copies, remote signals or barrier semaphores. Data moves between devices by JAX's collectives and lax.ppermute only.
A program may use at most 64 MiB of HBM per device.

```python
import math
import jax
import jax.numpy as jnp
from jax import lax

INPUTS = 1024
SAMPLES = 2048
TAPS = 4
CHANNELS = 32
FRAMES = 32
CHAN_FIRST = 496


def steps_of(own_key, shape, cuts, low, top_value):
    def one(position, shards_of):
        steps = jax.random.uniform(jax.random.fold_in(jax.random.fold_in(own_key, 6), position), (shards_of,), jnp.float32, low / len(cuts), top_value / len(cuts))
        return jnp.repeat(jnp.exp(steps), shape[position] // shards_of).reshape((-1,) + (1,) * (len(shape) - position - 1))

    factor_of = one(*cuts[0])
    for cut in cuts[1:]:
        factor_of = factor_of * one(*cut)
    return factor_of


def gaussian(own_key, dims, width, bound, shards=(), kind=jnp.bfloat16):
    entries = width * jax.random.normal(own_key, dims, jnp.float32)
    if shards:
        entries = entries * steps_of(own_key, dims, shards, -0.22, 0.18)
    return jnp.clip(entries, -bound, bound).astype(kind)


def setup_inputs(seed: int = 0) -> dict:
    key_list = jax.random.split(jax.random.key(seed), 4)
    voltages = gaussian(key_list[0], (INPUTS, FRAMES, SAMPLES), 1.0, 6.0, ((0, 32), (1, 8)))
    history = gaussian(key_list[1], (INPUTS, TAPS - 1, SAMPLES), 1.0, 6.0, ((0, 32),))
    window = gaussian(key_list[2], (TAPS, SAMPLES), TAPS ** -0.5, 3.0, (), jnp.float32)
    return dict(voltages=voltages, history=history, window=window)


def dft_table(channels, samples, first_bin):
    chan_bins = jnp.arange(channels, dtype=jnp.int32) + first_bin
    positions = jnp.arange(samples, dtype=jnp.int32)
    turns = chan_bins[:, None] * positions[None, :] % samples
    phases = turns.astype(jnp.float32) * (2.0 * math.pi / samples)
    scaling = 1.0 / math.sqrt(samples)
    return jnp.stack([jnp.cos(phases), -jnp.sin(phases)], axis=1) * scaling

def reference(voltages, history, window):
    weights = dft_table(CHANNELS, SAMPLES, CHAN_FIRST)
    block_inputs = min(INPUTS, 64)
    num_blocks = INPUTS // block_inputs

    def one_block(pair):
        volt_block, hist_block = pair
        extended = jnp.concatenate([hist_block, volt_block], axis=1).astype(jnp.float32)
        filtered = window[0] * extended[:, 0:FRAMES, :]
        for tap_index in range(1, TAPS):
            filtered = filtered + window[tap_index] * extended[:, tap_index:tap_index + FRAMES, :]
        return jnp.einsum('itn,cpn->citp', filtered, weights, precision=lax.Precision.HIGHEST)
    spectra = lax.map(one_block, (voltages.reshape(num_blocks, block_inputs, FRAMES, SAMPLES), history.reshape(num_blocks, block_inputs, TAPS - 1, SAMPLES)))
    spectra = jnp.moveaxis(spectra, 0, 1).reshape(CHANNELS, INPUTS, FRAMES, 2)

    def one_channel(chan_data):
        real_side = chan_data.transpose(1, 2, 0).reshape(2 * FRAMES, INPUTS)
        swapped = jnp.stack([chan_data[:, :, 1], -chan_data[:, :, 0]], axis=2)
        imag_side = swapped.transpose(1, 2, 0).reshape(2 * FRAMES, INPUTS)
        real_part = jnp.dot(real_side.T, real_side, precision=lax.Precision.HIGHEST)
        imag_part = jnp.dot(imag_side.T, real_side, precision=lax.Precision.HIGHEST)
        return jnp.stack([real_part, imag_part], axis=1)
    summed = lax.map(one_channel, spectra)
    return jnp.transpose(summed, (1, 0, 2, 3)) / FRAMES
```

```python
import math

import jax
import jax.numpy as jnp
import numpy as np
from jax import lax
from jax.experimental import pallas as pl
from jax.experimental.pallas import tpu as pltpu
from jax.sharding import PartitionSpec as P

TAPS = 4
SAMPLES = 2048
CHANNELS = 32
CHAN_FIRST = 496
IN_BLK = 32
FR_BLK = 4
FRQ = 8
LANES = 128


def dft_table():
    bins = np.arange(CHANNELS, dtype=np.int64) + CHAN_FIRST
    turns = bins[:, None] * np.arange(SAMPLES, dtype=np.int64)[None, :] % SAMPLES
    phases = turns * (2.0 * math.pi / SAMPLES)
    both = np.concatenate([np.cos(phases), -np.sin(phases)]) / math.sqrt(SAMPLES)
    return both.astype(np.float32)


def two_terms(x):
    high = x.astype(jnp.bfloat16)
    low = (x - high.astype(jnp.float32)).astype(jnp.bfloat16)
    return high, low


def transform_kernel(first_ref, volt_ref, hist_ref, window_ref, table_ref, out_ref, rows_ref):
    volts = volt_ref[...].reshape(FR_BLK * IN_BLK, SAMPLES)
    hist = hist_ref[...].reshape((TAPS - 1) * IN_BLK, SAMPLES)
    frames = jnp.concatenate([volts, hist, jnp.zeros((IN_BLK, SAMPLES), jnp.bfloat16)], axis=0)
    table = table_ref[...]
    lane = lax.broadcasted_iota(jnp.int32, (2 * CHANNELS, LANES), 1)
    first = first_ref[0] == 0
    own = jnp.zeros((2 * CHANNELS, LANES), jnp.float32)
    later = own
    past = own
    for tap in range(TAPS):
        high, low = two_terms(table * window_ref[tap : tap + 1, :])
        dims = (((1,), (1,)), ((), ()))
        part = lax.dot_general(high, frames, dims, preferred_element_type=jnp.float32)
        part = part + lax.dot_general(low, frames, dims, preferred_element_type=jnp.float32)
        moved = part[:, :LANES]
        split = (TAPS - 1 - tap) * IN_BLK
        if split:
            moved = pltpu.roll(moved, split, 1)
            later = later + jnp.where(lane < split, moved, 0.0)
            moved = jnp.where(lane < split, 0.0, moved)
            before = part[:, LANES:]
            if tap:
                before = pltpu.roll(before, LANES - tap * IN_BLK, 1)
            past = past + jnp.where(lane < split, before, 0.0)
        own = own + moved
    own = own + jnp.where(first, past, 0.0)
    for part in range(2):
        rows = slice(part * CHANNELS, (part + 1) * CHANNELS)
        rows_ref[pl.ds(2 * part, CHANNELS, 4), :] = own[rows]
        rows_ref[pl.ds(2 * part + 1, CHANNELS, 4), :] = later[rows]
    chunk = rows_ref[...]
    for copy in range(FRQ):
        out_ref[copy] = chunk


def gram_kernel(tile_ref, got_ref, out_ref, by_tile_ref):
    lane_group = lax.broadcasted_iota(jnp.int32, (8, LANES), 1) // IN_BLK
    spectra = {}
    for blk in range(FRQ):
        for kind in range(4):
            quads = [got_ref[pl.ds(blk * LANES + 4 * jj + kind, 8, 16), :] for jj in range(4)]
            for slot in range(4 if kind % 2 == 0 else 3):
                row = None
                for jj in range(4):
                    shift = (jj - slot) % 4 * IN_BLK
                    moved = pltpu.roll(quads[jj], shift, 1) if shift else quads[jj]
                    row = moved if row is None else jnp.where(lane_group == jj, moved, row)
                spectra[blk, kind // 2, kind % 2, slot] = row
    for part in range(2):
        for blk in range(FRQ):
            for slot in range(4):
                row = spectra[blk, part, 0, slot]
                if blk and slot < TAPS - 1:
                    row = row + spectra[blk - 1, part, 1, slot]
                k = (part * FRQ + blk) * FR_BLK + slot
                by_tile_ref[pl.ds(8 * k, 8), :] = row
    half = FRQ * FR_BLK
    tile = tile_ref[0]
    left = by_tile_ref[pl.ds(tile, 2 * half, 8), :] * (1.0 / half)
    left = jnp.concatenate([left, jnp.concatenate([left[half:], -left[:half]], axis=0)], axis=1)
    high, low = two_terms(left)
    left = jnp.concatenate([high, high, low], axis=0)
    for col in range(8):
        high, low = two_terms(by_tile_ref[pl.ds(col, 2 * half, 8), :])
        right = jnp.concatenate([high, low, high], axis=0)
        vis = lax.dot_general(left, right, (((0,), (0,)), ((), ())), preferred_element_type=jnp.float32)
        for part in range(2):
            out_ref[pl.ds(2 * col + part, LANES, 16), :] = vis[part * LANES : (part + 1) * LANES]


def body(voltages, history, window):
    place = lax.axis_index("frq").astype(jnp.int32).reshape(1)
    smem = pl.BlockSpec(memory_space=pltpu.SMEM)
    vmem = pl.BlockSpec(memory_space=pltpu.VMEM)
    chunks = pl.pallas_call(
        transform_kernel,
        out_shape=jax.ShapeDtypeStruct((FRQ, LANES, LANES), jnp.float32),
        in_specs=[smem, vmem, vmem, vmem, vmem],
        out_specs=vmem,
        scratch_shapes=[pltpu.VMEM((LANES, LANES), jnp.float32)],
        name="transform",
    )(place, voltages.transpose(1, 0, 2), history.transpose(1, 0, 2), window, jnp.asarray(dft_table()))
    chunks = chunks.reshape(FRQ * CHANNELS, 4, LANES)
    got = lax.all_to_all(chunks, ("frq", "inp"), 0, 0, tiled=True)
    rows = pl.pallas_call(
        gram_kernel,
        out_shape=jax.ShapeDtypeStruct((LANES * 16, LANES), jnp.float32),
        in_specs=[smem, vmem],
        out_specs=vmem,
        scratch_shapes=[pltpu.VMEM((2 * FRQ * FR_BLK * 8, LANES), jnp.float32)],
        name="gram",
    )(place, got.reshape(FRQ * LANES, LANES))
    return rows.reshape(LANES, 8, 2, LANES).transpose(0, 2, 1, 3).reshape(LANES, 1, 2, 8 * LANES)


def solution(mesh):
    return jax.shard_map(
        body,
        mesh=mesh,
        in_specs=(P("inp", "frq", None), P("inp", None, None), P()),
        out_specs=P("frq", "inp", None, None),
        check_vma=False,
    )
```

```python
import math

import jax
import jax.numpy as jnp
import numpy as np
from jax import lax
from jax.experimental import pallas as pl
from jax.experimental.pallas import tpu as pltpu
from jax.sharding import PartitionSpec as P

TAPS = 4
SAMPLES = 2048
CHANNELS = 32
CHAN_FIRST = 496
IN_BLK = 32
FR_BLK = 4
FRQ = 8
LANES = 128
STEP = 256
STEPS = SAMPLES // STEP
POWER = 16
TOP = 7


def dft_table():
    bins = np.arange(CHANNELS, dtype=np.int64) + CHAN_FIRST
    turns = bins[:, None] * np.arange(SAMPLES, dtype=np.int64)[None, :] % SAMPLES
    phases = turns * (2.0 * math.pi / SAMPLES)
    both = np.concatenate([np.cos(phases), -np.sin(phases)]) / math.sqrt(SAMPLES)
    return both.astype(np.float32)


def two_terms(x):
    high = x.astype(jnp.bfloat16)
    low = (x - high.astype(jnp.float32)).astype(jnp.bfloat16)
    return high, low


def transform_kernel(first_ref, volt_hbm, hist_hbm, window_ref, table_hbm, out_ref,
                     volt_ref, hist_ref, table_ref, rows_ref, sems):
    copies = []
    for step in range(STEPS):
        cols = pl.ds(step * STEP, STEP)
        moves = [(table_hbm.at[:, cols], table_ref.at[:, cols]), (hist_hbm.at[:, cols], hist_ref.at[:, cols])]
        for tile in range(step * STEP // LANES, (step + 1) * STEP // LANES):
            moves.append((volt_hbm.at[:, :, pl.ds(tile * LANES, LANES)], volt_ref.at[tile]))
        copies.append([pltpu.make_async_copy(*move, sems.at[step, i]) for i, move in enumerate(moves)])
        for copy in copies[-1]:
            copy.start()
    lane = lax.broadcasted_iota(jnp.int32, (2 * CHANNELS, LANES), 1)
    frame = lane % FR_BLK
    zeros = jnp.zeros((IN_BLK, STEP), jnp.bfloat16)
    dims = (((1,), (1,)), ((), ()))
    total = None
    for step in range(STEPS):
        for copy in copies[step]:
            copy.wait()
        cols = slice(step * STEP, (step + 1) * STEP)
        tiles = range(step * STEP // LANES, (step + 1) * STEP // LANES)
        volts = jnp.concatenate([volt_ref.at[tile].reshape(LANES, LANES)[...] for tile in tiles], axis=1)
        frames = jnp.concatenate([volts, hist_ref[:, cols], zeros], axis=0)
        table = table_ref[:, cols]
        weights = jnp.concatenate([table * window_ref[tap : tap + 1, cols] for tap in range(TAPS)], axis=0)
        high, low = two_terms(weights)
        part = lax.dot_general(high, frames, dims, preferred_element_type=jnp.float32)
        part = part + lax.dot_general(low, frames, dims, preferred_element_type=jnp.float32)
        total = part if total is None else total + part
    own = jnp.zeros((2 * CHANNELS, LANES), jnp.float32)
    later = own
    past = own
    for tap in range(TAPS):
        part = total[tap * 2 * CHANNELS : (tap + 1) * 2 * CHANNELS]
        here = part[:, :LANES]
        moved = TAPS - 1 - tap
        if moved == 0:
            own = own + here
            continue
        own = own + jnp.where(frame < moved, 0.0, pltpu.roll(here, moved, 1))
        later = later + jnp.where(frame < moved, pltpu.roll(here, LANES - FR_BLK + moved, 1), 0.0)
        before = part[:, LANES:]
        if tap:
            before = pltpu.roll(before, LANES - tap * IN_BLK, 1)
        past = past + jnp.where(lane < moved * IN_BLK, before, 0.0)
    row = lax.broadcasted_iota(jnp.int32, (LANES, LANES), 0)
    col = lax.broadcasted_iota(jnp.int32, (LANES, LANES), 1)
    order = jnp.where(col == row % FR_BLK * IN_BLK + row // FR_BLK, 1.0, 0.0).astype(jnp.bfloat16)
    high, low = two_terms(jnp.concatenate([own, later], axis=0))
    sorted_rows = jnp.dot(high, order, preferred_element_type=jnp.float32)
    sorted_rows = sorted_rows + jnp.dot(low, order, preferred_element_type=jnp.float32)
    own = sorted_rows[: 2 * CHANNELS] + jnp.where(first_ref[0] == 0, past, 0.0)
    later = sorted_rows[2 * CHANNELS :]
    quads = [own[:CHANNELS], later[:CHANNELS], own[CHANNELS:], later[CHANNELS:]]
    top = jnp.maximum(jnp.maximum(jnp.abs(quads[0]), jnp.abs(quads[1])), jnp.maximum(jnp.abs(quads[2]), jnp.abs(quads[3])))
    top = jnp.maximum(jnp.max(top, axis=1, keepdims=True), 2.0**-100)
    shift = jnp.broadcast_to(jnp.ceil(jnp.log2(top)) - TOP, (CHANNELS, LANES))
    factor = jnp.exp2(-shift)
    lane = lane[:CHANNELS]
    for kind in range(4):
        value = quads[kind] * factor
        power = value * value
        power = power * power
        power = power * power
        power = power * power
        value = jnp.where(value < 0.0, -power, power)
        if kind % 2:
            value = jnp.where(lane < (TAPS - 1) * IN_BLK, value, shift)
        rows_ref[pl.ds(kind, CHANNELS, 4), :] = value
    chunk = rows_ref[...].astype(jnp.bfloat16)
    for copy in range(FRQ):
        out_ref[copy] = chunk


def gram_kernel(tile_ref, got_ref, out_ref, wide_ref, by_tile_ref):
    wide_ref[...] = got_ref[...].astype(jnp.float32)
    lane_group = lax.broadcasted_iota(jnp.int32, (8, LANES), 1) // IN_BLK
    spectra = {}
    for blk in range(FRQ):
        quads = [[wide_ref[pl.ds(blk * LANES + 4 * jj + kind, 8, 16), :] for kind in range(4)] for jj in range(4)]
        for jj in range(4):
            shift = jnp.broadcast_to(quads[jj][1][:, LANES - 1 :], (8, LANES))
            for kind in range(4):
                code = quads[jj][kind]
                value = jnp.exp2(jnp.log2(jnp.abs(code)) * (1.0 / POWER) + shift)
                quads[jj][kind] = jnp.where(code < 0.0, -value, value)
        for kind in range(4):
            for slot in range(4 if kind % 2 == 0 else 3):
                row = None
                for jj in range(4):
                    shift = (jj - slot) % 4 * IN_BLK
                    moved = pltpu.roll(quads[jj][kind], shift, 1) if shift else quads[jj][kind]
                    row = moved if row is None else jnp.where(lane_group == jj, moved, row)
                spectra[blk, kind // 2, kind % 2, slot] = row
    for part in range(2):
        for blk in range(FRQ):
            for slot in range(4):
                row = spectra[blk, part, 0, slot]
                if blk and slot < TAPS - 1:
                    row = row + spectra[blk - 1, part, 1, slot]
                k = (part * FRQ + blk) * FR_BLK + slot
                by_tile_ref[pl.ds(8 * k, 8), :] = row
    half = FRQ * FR_BLK
    tile = tile_ref[0]
    left = by_tile_ref[pl.ds(tile, 2 * half, 8), :] * (1.0 / half)
    left = jnp.concatenate([left, jnp.concatenate([left[half:], -left[:half]], axis=0)], axis=1)
    high, low = two_terms(left)
    left = jnp.concatenate([high, high, low], axis=0)
    for col in range(8):
        high, low = two_terms(by_tile_ref[pl.ds(col, 2 * half, 8), :])
        right = jnp.concatenate([high, low, high], axis=0)
        vis = lax.dot_general(left, right, (((0,), (0,)), ((), ())), preferred_element_type=jnp.float32)
        for part in range(2):
            out_ref[pl.ds(2 * col + part, LANES, 16), :] = vis[part * LANES : (part + 1) * LANES]


def body(voltages, history, window):
    place = lax.axis_index("frq").astype(jnp.int32).reshape(1)
    smem = pl.BlockSpec(memory_space=pltpu.SMEM)
    vmem = pl.BlockSpec(memory_space=pltpu.VMEM)
    hbm = pl.BlockSpec(memory_space=pl.ANY)
    past = history.transpose(1, 0, 2).reshape((TAPS - 1) * IN_BLK, SAMPLES)
    chunks = pl.pallas_call(
        transform_kernel,
        out_shape=jax.ShapeDtypeStruct((FRQ, LANES, LANES), jnp.bfloat16),
        in_specs=[smem, hbm, hbm, vmem, hbm],
        out_specs=vmem,
        scratch_shapes=[
            pltpu.VMEM((SAMPLES // LANES, IN_BLK, FR_BLK, LANES), jnp.bfloat16),
            pltpu.VMEM(past.shape, jnp.bfloat16),
            pltpu.VMEM((2 * CHANNELS, SAMPLES), jnp.float32),
            pltpu.VMEM((LANES, LANES), jnp.float32),
            pltpu.SemaphoreType.DMA((STEPS, 2 + STEP // LANES)),
        ],
        name="transform",
    )(place, voltages, past, window, jnp.asarray(dft_table()))
    chunks = chunks.reshape(FRQ * CHANNELS, 4, LANES)
    got = lax.all_to_all(chunks, ("frq", "inp"), 0, 0, tiled=True)
    rows = pl.pallas_call(
        gram_kernel,
        out_shape=jax.ShapeDtypeStruct((LANES * 16, LANES), jnp.float32),
        in_specs=[smem, vmem],
        out_specs=vmem,
        scratch_shapes=[
            pltpu.VMEM((FRQ * LANES, LANES), jnp.float32),
            pltpu.VMEM((2 * FRQ * FR_BLK * 8, LANES), jnp.float32),
        ],
        name="gram",
    )(place, got.reshape(FRQ * LANES, LANES))
    return rows.reshape(LANES, 8, 2, LANES).transpose(0, 2, 1, 3).reshape(LANES, 1, 2, 8 * LANES)


def solution(mesh):
    return jax.shard_map(
        body,
        mesh=mesh,
        in_specs=(P("inp", "frq", None), P("inp", None, None), P()),
        out_specs=P("frq", "inp", None, None),
        check_vma=False,
    )
```

```python
import math

import jax
import jax.numpy as jnp
import numpy as np
from jax import lax
from jax.experimental import pallas as pl
from jax.experimental.pallas import tpu as pltpu
from jax.sharding import PartitionSpec as P

TAPS = 4
SAMPLES = 2048
CHANNELS = 32
CHAN_FIRST = 496
IN_BLK = 32
FR_BLK = 4
FRQ = 8
LANES = 128
STEP = 2048
STEPS = SAMPLES // STEP
POWER = 16
TOP = 7


def dft_table():
    bins = np.arange(CHANNELS, dtype=np.int64) + CHAN_FIRST
    turns = bins[:, None] * np.arange(SAMPLES, dtype=np.int64)[None, :] % SAMPLES
    phases = turns * (2.0 * math.pi / SAMPLES)
    both = np.concatenate([np.cos(phases), -np.sin(phases)]) / math.sqrt(SAMPLES)
    return both.astype(np.float32)


def two_terms(x):
    high = x.astype(jnp.bfloat16)
    low = (x - high.astype(jnp.float32)).astype(jnp.bfloat16)
    return high, low


def transform_kernel(first_ref, volt_hbm, hist_hbm, window_ref, table_hbm, out_ref,
                     volt_ref, hist_ref, table_ref, rows_ref, sems):
    copies = []
    for step in range(STEPS):
        cols = pl.ds(step * STEP, STEP)
        moves = [(table_hbm.at[:, cols], table_ref.at[:, cols]), (hist_hbm.at[:, cols], hist_ref.at[:, cols])]
        for tile in range(step * STEP // LANES, (step + 1) * STEP // LANES):
            moves.append((volt_hbm.at[:, :, pl.ds(tile * LANES, LANES)], volt_ref.at[tile]))
        copies.append([pltpu.make_async_copy(*move, sems.at[step, i]) for i, move in enumerate(moves)])
        for copy in copies[-1]:
            copy.start()
    lane = lax.broadcasted_iota(jnp.int32, (2 * CHANNELS, LANES), 1)
    frame = lane % FR_BLK
    zeros = jnp.zeros((IN_BLK, STEP), jnp.bfloat16)
    dims = (((1,), (1,)), ((), ()))
    total = None
    for step in range(STEPS):
        for copy in copies[step]:
            copy.wait()
        cols = slice(step * STEP, (step + 1) * STEP)
        tiles = range(step * STEP // LANES, (step + 1) * STEP // LANES)
        volts = jnp.concatenate([volt_ref.at[tile].reshape(LANES, LANES)[...] for tile in tiles], axis=1)
        frames = jnp.concatenate([volts, hist_ref[:, cols], zeros], axis=0)
        table = table_ref[:, cols]
        weights = jnp.concatenate([table * window_ref[tap : tap + 1, cols] for tap in range(TAPS)], axis=0)
        high, low = two_terms(weights)
        part = lax.dot_general(high, frames, dims, preferred_element_type=jnp.float32)
        part = part + lax.dot_general(low, frames, dims, preferred_element_type=jnp.float32)
        total = part if total is None else total + part
    own = jnp.zeros((2 * CHANNELS, LANES), jnp.float32)
    later = own
    past = own
    for tap in range(TAPS):
        part = total[tap * 2 * CHANNELS : (tap + 1) * 2 * CHANNELS]
        here = part[:, :LANES]
        moved = TAPS - 1 - tap
        if moved == 0:
            own = own + here
            continue
        own = own + jnp.where(frame < moved, 0.0, pltpu.roll(here, moved, 1))
        later = later + jnp.where(frame < moved, pltpu.roll(here, LANES - FR_BLK + moved, 1), 0.0)
        before = part[:, LANES:]
        if tap:
            before = pltpu.roll(before, LANES - tap * IN_BLK, 1)
        past = past + jnp.where(lane < moved * IN_BLK, before, 0.0)
    row = lax.broadcasted_iota(jnp.int32, (LANES, LANES), 0)
    col = lax.broadcasted_iota(jnp.int32, (LANES, LANES), 1)
    order = jnp.where(col == row % FR_BLK * IN_BLK + row // FR_BLK, 1.0, 0.0).astype(jnp.bfloat16)
    high, low = two_terms(jnp.concatenate([own, later], axis=0))
    sorted_rows = jnp.dot(high, order, preferred_element_type=jnp.float32)
    sorted_rows = sorted_rows + jnp.dot(low, order, preferred_element_type=jnp.float32)
    own = sorted_rows[: 2 * CHANNELS] + jnp.where(first_ref[0] == 0, past, 0.0)
    later = sorted_rows[2 * CHANNELS :]
    quads = [own[:CHANNELS], later[:CHANNELS], own[CHANNELS:], later[CHANNELS:]]
    top = jnp.maximum(jnp.maximum(jnp.abs(quads[0]), jnp.abs(quads[1])), jnp.maximum(jnp.abs(quads[2]), jnp.abs(quads[3])))
    top = jnp.maximum(jnp.max(top, axis=1, keepdims=True), 2.0**-100)
    shift = jnp.broadcast_to(jnp.ceil(jnp.log2(top)) - TOP, (CHANNELS, LANES))
    factor = jnp.exp2(-shift)
    lane = lane[:CHANNELS]
    for kind in range(4):
        value = quads[kind] * factor
        power = value * value
        power = power * power
        power = power * power
        power = power * power
        value = jnp.where(value < 0.0, -power, power)
        if kind % 2:
            value = jnp.where(lane < (TAPS - 1) * IN_BLK, value, shift)
        rows_ref[pl.ds(kind, CHANNELS, 4), :] = value
    chunk = rows_ref[...].astype(jnp.bfloat16)
    for copy in range(FRQ):
        out_ref[copy] = chunk


def gram_kernel(tile_ref, got_ref, out_ref, wide_ref, by_tile_ref):
    wide_ref[...] = got_ref[...].astype(jnp.float32)
    lane_group = lax.broadcasted_iota(jnp.int32, (8, LANES), 1) // IN_BLK
    spectra = {}
    for blk in range(FRQ):
        quads = [[wide_ref[pl.ds(blk * LANES + 4 * jj + kind, 8, 16), :] for kind in range(4)] for jj in range(4)]
        for jj in range(4):
            shift = jnp.broadcast_to(quads[jj][1][:, LANES - 1 :], (8, LANES))
            for kind in range(4):
                code = quads[jj][kind]
                value = jnp.exp2(jnp.log2(jnp.abs(code)) * (1.0 / POWER) + shift)
                quads[jj][kind] = jnp.where(code < 0.0, -value, value)
        for kind in range(4):
            for slot in range(4 if kind % 2 == 0 else 3):
                row = None
                for jj in range(4):
                    shift = (jj - slot) % 4 * IN_BLK
                    moved = pltpu.roll(quads[jj][kind], shift, 1) if shift else quads[jj][kind]
                    row = moved if row is None else jnp.where(lane_group == jj, moved, row)
                spectra[blk, kind // 2, kind % 2, slot] = row
    for part in range(2):
        for blk in range(FRQ):
            for slot in range(4):
                row = spectra[blk, part, 0, slot]
                if blk and slot < TAPS - 1:
                    row = row + spectra[blk - 1, part, 1, slot]
                k = (part * FRQ + blk) * FR_BLK + slot
                by_tile_ref[pl.ds(8 * k, 8), :] = row
    half = FRQ * FR_BLK
    tile = tile_ref[0]
    left = by_tile_ref[pl.ds(tile, 2 * half, 8), :] * (1.0 / half)
    left = jnp.concatenate([left, jnp.concatenate([left[half:], -left[:half]], axis=0)], axis=1)
    high, low = two_terms(left)
    left = jnp.concatenate([high, high, low], axis=0)
    for col in range(8):
        high, low = two_terms(by_tile_ref[pl.ds(col, 2 * half, 8), :])
        right = jnp.concatenate([high, low, high], axis=0)
        vis = lax.dot_general(left, right, (((0,), (0,)), ((), ())), preferred_element_type=jnp.float32)
        for part in range(2):
            out_ref[pl.ds(2 * col + part, LANES, 16), :] = vis[part * LANES : (part + 1) * LANES]


def body(voltages, history, window):
    place = lax.axis_index("frq").astype(jnp.int32).reshape(1)
    smem = pl.BlockSpec(memory_space=pltpu.SMEM)
    vmem = pl.BlockSpec(memory_space=pltpu.VMEM)
    hbm = pl.BlockSpec(memory_space=pl.ANY)
    past = history.transpose(1, 0, 2).reshape((TAPS - 1) * IN_BLK, SAMPLES)
    chunks = pl.pallas_call(
        transform_kernel,
        out_shape=pltpu.VMEM((FRQ, LANES, LANES), jnp.bfloat16),
        in_specs=[smem, hbm, hbm, vmem, hbm],
        out_specs=vmem,
        scratch_shapes=[
            pltpu.VMEM((SAMPLES // LANES, IN_BLK, FR_BLK, LANES), jnp.bfloat16),
            pltpu.VMEM(past.shape, jnp.bfloat16),
            pltpu.VMEM((2 * CHANNELS, SAMPLES), jnp.float32),
            pltpu.VMEM((LANES, LANES), jnp.float32),
            pltpu.SemaphoreType.DMA((STEPS, 2 + STEP // LANES)),
        ],
        name="transform",
    )(place, voltages, past, window, jnp.asarray(dft_table()))
    chunks = chunks.reshape(FRQ * CHANNELS, 4, LANES)
    got = lax.all_to_all(chunks, ("frq", "inp"), 0, 0, tiled=True)
    rows = pl.pallas_call(
        gram_kernel,
        out_shape=jax.ShapeDtypeStruct((LANES * 16, LANES), jnp.float32),
        in_specs=[smem, vmem],
        out_specs=vmem,
        scratch_shapes=[
            pltpu.VMEM((FRQ * LANES, LANES), jnp.float32),
            pltpu.VMEM((2 * FRQ * FR_BLK * 8, LANES), jnp.float32),
        ],
        name="gram",
    )(place, pltpu.with_memory_space_constraint(got.reshape(FRQ * LANES, LANES), pltpu.VMEM))
    return rows.reshape(LANES, 8, 2, LANES).transpose(0, 2, 1, 3).reshape(LANES, 1, 2, 8 * LANES)


def solution(mesh):
    return jax.shard_map(
        body,
        mesh=mesh,
        in_specs=(P("inp", "frq", None), P("inp", None, None), P()),
        out_specs=P("frq", "inp", None, None),
        check_vma=False,
    )
```

```python
import math

import jax
import jax.numpy as jnp
import numpy as np
from jax import lax
from jax.experimental import pallas as pl
from jax.experimental.pallas import tpu as pltpu
from jax.sharding import PartitionSpec as P

TAPS = 4
SAMPLES = 2048
CHANNELS = 32
CHAN_FIRST = 496
IN_BLK = 32
FR_BLK = 4
FRQ = 8
LANES = 128
STEP = 256
POWER = 16
TOP = 7


def dft_table():
    bins = np.arange(CHANNELS, dtype=np.int64) + CHAN_FIRST
    turns = bins[:, None] * np.arange(SAMPLES, dtype=np.int64)[None, :] % SAMPLES
    phases = turns * (2.0 * math.pi / SAMPLES)
    both = np.concatenate([np.cos(phases), -np.sin(phases)]) / math.sqrt(SAMPLES)
    return both.astype(np.float32)


def two_terms(x):
    high = x.astype(jnp.bfloat16)
    low = (x - high.astype(jnp.float32)).astype(jnp.bfloat16)
    return high, low


def transform_kernel(volt_hbm, hist_hbm, window_hbm, table_hbm, out_ref,
                     volt_ref, hist_ref, window_ref, table_ref, rows_ref, sems):
    tiles = SAMPLES // LANES
    pltpu.make_async_copy(window_hbm, window_ref, sems.at[0]).start()
    pltpu.make_async_copy(table_hbm, table_ref, sems.at[1]).start()
    for tile in range(tiles):
        pltpu.make_async_copy(volt_hbm.at[:, :, pl.ds(tile * LANES, LANES)], volt_ref.at[tile], sems.at[2]).start()
    pltpu.make_async_copy(hist_hbm, hist_ref, sems.at[3]).start()
    pltpu.make_async_copy(window_hbm, window_ref, sems.at[0]).wait()
    pltpu.make_async_copy(table_hbm, table_ref, sems.at[1]).wait()
    pltpu.make_async_copy(volt_ref, volt_ref, sems.at[2]).wait()
    pltpu.make_async_copy(hist_hbm, hist_ref, sems.at[3]).wait()
    lane = lax.broadcasted_iota(jnp.int32, (2 * CHANNELS, LANES), 1)
    frame = lane % FR_BLK
    zeros = jnp.zeros((IN_BLK, STEP), jnp.bfloat16)
    dims = (((1,), (1,)), ((), ()))
    total = None
    for step in range(SAMPLES // STEP):
        cols = slice(step * STEP, (step + 1) * STEP)
        span = range(step * STEP // LANES, (step + 1) * STEP // LANES)
        volts = jnp.concatenate([volt_ref.at[tile].reshape(LANES, LANES)[...] for tile in span], axis=1)
        frames = jnp.concatenate([volts, hist_ref[:, cols], zeros], axis=0)
        table = table_ref[:, cols]
        weights = jnp.concatenate([table * window_ref[tap : tap + 1, cols] for tap in range(TAPS)], axis=0)
        high, low = two_terms(weights)
        part = lax.dot_general(high, frames, dims, preferred_element_type=jnp.float32)
        part = part + lax.dot_general(low, frames, dims, preferred_element_type=jnp.float32)
        total = part if total is None else total + part
    own = jnp.zeros((2 * CHANNELS, LANES), jnp.float32)
    later = own
    past = own
    for tap in range(TAPS):
        part = total[tap * 2 * CHANNELS : (tap + 1) * 2 * CHANNELS]
        here = part[:, :LANES]
        moved = TAPS - 1 - tap
        if moved == 0:
            own = own + here
            continue
        own = own + jnp.where(frame < moved, 0.0, pltpu.roll(here, moved, 1))
        later = later + jnp.where(frame < moved, pltpu.roll(here, LANES - FR_BLK + moved, 1), 0.0)
        before = part[:, LANES:]
        if tap:
            before = pltpu.roll(before, LANES - tap * IN_BLK, 1)
        past = past + jnp.where(lane < moved * IN_BLK, before, 0.0)
    row = lax.broadcasted_iota(jnp.int32, (LANES, LANES), 0)
    col = lax.broadcasted_iota(jnp.int32, (LANES, LANES), 1)
    order = jnp.where(col == row % FR_BLK * IN_BLK + row // FR_BLK, 1.0, 0.0).astype(jnp.bfloat16)
    high, low = two_terms(jnp.concatenate([own, later], axis=0))
    sorted_rows = jnp.dot(high, order, preferred_element_type=jnp.float32)
    sorted_rows = sorted_rows + jnp.dot(low, order, preferred_element_type=jnp.float32)
    own = sorted_rows[: 2 * CHANNELS] + jnp.where(lax.axis_index("frq") == 0, past, 0.0)
    later = sorted_rows[2 * CHANNELS :]
    quads = [own[:CHANNELS], own[CHANNELS:], later[:CHANNELS], later[CHANNELS:]]
    top = jnp.maximum(jnp.maximum(jnp.abs(quads[0]), jnp.abs(quads[1])), jnp.maximum(jnp.abs(quads[2]), jnp.abs(quads[3])))
    top = jnp.maximum(jnp.max(top, axis=1, keepdims=True), 2.0**-100)
    shift = jnp.broadcast_to(jnp.ceil(jnp.log2(top)) - TOP, (CHANNELS, LANES))
    factor = jnp.exp2(-shift)
    lane = lane[:CHANNELS]
    for kind in range(4):
        value = quads[kind] * factor
        power = value * value
        power = power * power
        power = power * power
        power = power * power
        value = jnp.where(value < 0.0, -power, power)
        if kind >= 2:
            value = jnp.where(lane < (TAPS - 1) * IN_BLK, value, shift)
        value = pltpu.roll(value, lax.axis_index("inp") % 4 * IN_BLK, 1)
        for copy in range(2):
            rows_ref[pl.ds(4 * copy + kind, CHANNELS, 8), :] = value
    for chan in range(CHANNELS):
        twice = rows_ref[8 * chan : 8 * chan + 8, :]
        chunk = jnp.concatenate([twice, twice], axis=0).astype(jnp.bfloat16)
        for copy in range(FRQ // 4):
            out_ref[pl.ds(4 * FRQ * chan + 16 * copy, 16), :] = chunk


def frames_of(got_ref, first_row):
    rows = 4 * FRQ
    lane_group = lax.broadcasted_iota(jnp.int32, (rows, LANES), 1) // IN_BLK
    row = lax.broadcasted_iota(jnp.int32, (rows, LANES), 0)
    upper = row % 4 >= 2
    quarters = [got_ref[pl.ds(first_row + rows * g, rows), :].astype(jnp.float32) for g in range(4)]
    codes = []
    for slot in range(4):
        code = quarters[-slot % 4]
        for group in range(1, 4):
            code = jnp.where(lane_group == group, quarters[(group - slot) % 4], code)
        codes.append(pltpu.roll(code, LANES - slot * IN_BLK, 1) if slot else code)
    shift = jnp.where(upper, codes[3], pltpu.roll(codes[3], rows - 2, 0))
    values = []
    for slot in range(4):
        value = jnp.exp2(jnp.log2(jnp.abs(codes[slot])) * (1.0 / POWER) + shift)
        value = jnp.where(codes[slot] < 0.0, -value, value)
        if slot < TAPS - 1:
            value = value + jnp.where(row < 2, 0.0, pltpu.roll(value, 2, 0))
        values.append(value)
    pairs = [jnp.where(upper, pltpu.roll(values[i + 1], 2, 0), values[i]) for i in (0, 2)]
    return jnp.concatenate(pairs, axis=0)


def gram_kernel(got_ref, out_hbm, vis_ref, sems):
    left = frames_of(got_ref, lax.axis_index("frq") * LANES) * (1.0 / (FRQ * FR_BLK))
    real = lax.broadcasted_iota(jnp.int32, left.shape, 0) % 2 == 0
    turned = jnp.where(real, pltpu.roll(left, left.shape[0] - 1, 0), -pltpu.roll(left, 1, 0))
    high, low = two_terms(jnp.concatenate([left, turned], axis=1))
    left = jnp.concatenate([high, high, low], axis=0)
    row = lax.broadcasted_iota(jnp.int32, (2 * LANES, 2 * LANES), 0)
    col = lax.broadcasted_iota(jnp.int32, (2 * LANES, 2 * LANES), 1)
    order = jnp.where(col == row % 2 * LANES + row // 2, 1.0, 0.0).astype(jnp.bfloat16)
    left = lax.dot_general(order, left, (((1,), (1,)), ((), ())), preferred_element_type=jnp.float32)
    left = left.astype(jnp.bfloat16)
    copies = []
    for pair in range(4):
        high, low = two_terms(jnp.concatenate([frames_of(got_ref, (2 * pair + i) * LANES) for i in range(2)], axis=1))
        right = jnp.concatenate([high, low, high], axis=0)
        vis = jnp.dot(left, right, preferred_element_type=jnp.float32)
        for i in range(2):
            tile = 2 * pair + i
            vis_ref.at[tile].reshape(2 * LANES, LANES)[...] = vis[:, i * LANES : (i + 1) * LANES]
            copies.append(pltpu.make_async_copy(vis_ref.at[tile], out_hbm.at[:, tile], sems.at[tile]))
            copies[-1].start()
    for copy in copies:
        copy.wait()


def body(voltages, history, window):
    vmem = pl.BlockSpec(memory_space=pltpu.VMEM)
    hbm = pl.BlockSpec(memory_space=pl.ANY)
    past = history.transpose(1, 0, 2).reshape((TAPS - 1) * IN_BLK, SAMPLES)
    chunks = pl.pallas_call(
        transform_kernel,
        out_shape=pltpu.VMEM((FRQ * LANES, LANES), jnp.bfloat16),
        in_specs=[hbm] * 4,
        out_specs=vmem,
        scratch_shapes=[
            pltpu.VMEM((SAMPLES // LANES, IN_BLK, FR_BLK, LANES), jnp.bfloat16),
            pltpu.VMEM(past.shape, jnp.bfloat16),
            pltpu.VMEM(window.shape, jnp.float32),
            pltpu.VMEM((2 * CHANNELS, SAMPLES), jnp.float32),
            pltpu.VMEM((2 * LANES, LANES), jnp.float32),
            pltpu.SemaphoreType.DMA((4,)),
        ],
        name="transform",
    )(voltages, past, window, jnp.asarray(dft_table()))
    chunks = chunks.reshape(FRQ * CHANNELS, 4, LANES)
    got = lax.all_to_all(chunks, ("inp", "frq"), 0, 0, tiled=True)
    got = pltpu.with_memory_space_constraint(got.reshape(FRQ * LANES, LANES), pltpu.VMEM)
    tiles = pl.pallas_call(
        gram_kernel,
        out_shape=jax.ShapeDtypeStruct((LANES, 8, 2, LANES), jnp.float32),
        in_specs=[vmem],
        out_specs=hbm,
        scratch_shapes=[pltpu.VMEM((8, LANES, 2, LANES), jnp.float32), pltpu.SemaphoreType.DMA((8,))],
        name="gram",
    )(got)
    return tiles.transpose(0, 2, 1, 3).reshape(LANES, 1, 2, 8 * LANES)


def solution(mesh):
    return jax.shard_map(
        body,
        mesh=mesh,
        in_specs=(P("inp", "frq", None), P("inp", None, None), P()),
        out_specs=P("frq", "inp", None, None),
        check_vma=False,
    )
```

```python
import math

import jax
import jax.numpy as jnp
import numpy as np
from jax import lax
from jax.experimental import pallas as pl
from jax.experimental.pallas import tpu as pltpu
from jax.sharding import PartitionSpec as P

TAPS = 4
SAMPLES = 2048
CHANNELS = 32
CHAN_FIRST = 496
IN_BLK = 32
FR_BLK = 4
FRQ = 8
LANES = 128
STEP = 256
POWER = 16
TOP = 7


def dft_table():
    bins = np.arange(CHANNELS, dtype=np.int64) + CHAN_FIRST
    turns = bins[:, None] * np.arange(SAMPLES, dtype=np.int64)[None, :] % SAMPLES
    phases = turns * (2.0 * math.pi / SAMPLES)
    both = np.concatenate([np.cos(phases), -np.sin(phases)]) / math.sqrt(SAMPLES)
    return both.astype(np.float32)


def two_terms(x):
    high = x.astype(jnp.bfloat16)
    low = (x - high.astype(jnp.float32)).astype(jnp.bfloat16)
    return high, low


def products(table_ref, window_ref, taps, frames_at):
    dims = (((1,), (1,)), ((), ()))
    total = None
    for step in range(SAMPLES // STEP):
        cols = slice(step * STEP, (step + 1) * STEP)
        table = table_ref[:, cols]
        weights = jnp.concatenate([table * window_ref[tap : tap + 1, cols] for tap in range(taps)], axis=0)
        high, low = two_terms(weights)
        frames = frames_at(step)
        part = lax.dot_general(high, frames, dims, preferred_element_type=jnp.float32)
        part = part + lax.dot_general(low, frames, dims, preferred_element_type=jnp.float32)
        total = part if total is None else total + part
    return [total[tap * 2 * CHANNELS : (tap + 1) * 2 * CHANNELS] for tap in range(taps)]


def transform_kernel(volt_hbm, hist_hbm, window_hbm, table_hbm, out_ref,
                     volt_ref, hist_ref, window_ref, table_ref, rows_ref, past_ref, sems):
    first = (lax.axis_index("y") == 0) & (lax.axis_index("zh") == 0)
    hist_copy = pltpu.make_async_copy(hist_hbm, hist_ref, sems.at[3])
    pltpu.make_async_copy(window_hbm, window_ref, sems.at[0]).start()
    pltpu.make_async_copy(table_hbm, table_ref, sems.at[1]).start()
    for tile in range(SAMPLES // LANES):
        pltpu.make_async_copy(volt_hbm.at[:, :, pl.ds(tile * LANES, LANES)], volt_ref.at[tile], sems.at[2]).start()
    lane = lax.broadcasted_iota(jnp.int32, (2 * CHANNELS, LANES), 1)
    past_ref[...] = jnp.zeros((2 * CHANNELS, LANES), jnp.float32)
    pltpu.make_async_copy(window_hbm, window_ref, sems.at[0]).wait()
    pltpu.make_async_copy(table_hbm, table_ref, sems.at[1]).wait()

    @pl.when(first)
    def _():
        hist_copy.start()
        hist_copy.wait()

        def frames_at(step):
            rows = hist_ref[:, step * STEP : (step + 1) * STEP]
            return jnp.concatenate([rows, jnp.zeros((IN_BLK, STEP), jnp.bfloat16)], axis=0)

        past = jnp.zeros((2 * CHANNELS, LANES), jnp.float32)
        for tap, before in enumerate(products(table_ref, window_ref, TAPS - 1, frames_at)):
            if tap:
                before = pltpu.roll(before, LANES - tap * IN_BLK, 1)
            past = past + jnp.where(lane < (TAPS - 1 - tap) * IN_BLK, before, 0.0)
        past_ref[...] = past

    pltpu.make_async_copy(volt_ref, volt_ref, sems.at[2]).wait()

    def frames_at(step):
        tiles = range(step * STEP // LANES, (step + 1) * STEP // LANES)
        return jnp.concatenate([volt_ref.at[tile].reshape(LANES, LANES)[...] for tile in tiles], axis=1)

    frame = lane % FR_BLK
    own = later = None
    for tap, here in enumerate(products(table_ref, window_ref, TAPS, frames_at)):
        moved = TAPS - 1 - tap
        if moved == 0:
            own = own + here
            continue
        kept = jnp.where(frame < moved, 0.0, pltpu.roll(here, moved, 1))
        passed = jnp.where(frame < moved, pltpu.roll(here, LANES - FR_BLK + moved, 1), 0.0)
        own = kept if own is None else own + kept
        later = passed if later is None else later + passed
    past = past_ref[...]
    top = jnp.maximum(jnp.maximum(jnp.abs(own), jnp.abs(later)), jnp.abs(past))
    top = jnp.maximum(top[:CHANNELS], top[CHANNELS:])
    top = jnp.maximum(jnp.max(top, axis=1, keepdims=True), 2.0**-100)
    shift = jnp.broadcast_to(jnp.ceil(jnp.log2(top)) - (TOP - 1), (CHANNELS, LANES))
    factor = jnp.exp2(-shift)
    row = lax.broadcasted_iota(jnp.int32, (LANES, LANES), 0)
    col = lax.broadcasted_iota(jnp.int32, (LANES, LANES), 1)
    order = jnp.where(col == row % FR_BLK * IN_BLK + row // FR_BLK, 1.0, 0.0).astype(jnp.bfloat16)
    high, low = two_terms(jnp.concatenate([own, later], axis=0))
    sorted_rows = jnp.dot(high, order, preferred_element_type=jnp.float32)
    sorted_rows = sorted_rows + jnp.dot(low, order, preferred_element_type=jnp.float32)
    own = sorted_rows[: 2 * CHANNELS] + past
    later = sorted_rows[2 * CHANNELS :]
    quads = [own[:CHANNELS], own[CHANNELS:], later[:CHANNELS], later[CHANNELS:]]
    lane = lane[:CHANNELS]
    for kind in range(4):
        value = quads[kind] * factor
        power = value * value
        power = power * power
        power = power * power
        power = power * power
        value = jnp.where(value < 0.0, -power, power)
        if kind >= 2:
            value = jnp.where(lane < (TAPS - 1) * IN_BLK, value, shift)
        value = pltpu.roll(value, (lax.axis_index("zl") % 2 * 2 + lax.axis_index("c")) * IN_BLK, 1)
        for copy in range(2):
            rows_ref[pl.ds(4 * copy + kind, CHANNELS, 8), :] = value
    out_ref[...] = rows_ref[...].astype(jnp.bfloat16)


def frames_of(blocks, tile):
    rows = 4 * FRQ
    lane_group = lax.broadcasted_iota(jnp.int32, (8, LANES), 1) // IN_BLK
    row = lax.broadcasted_iota(jnp.int32, (rows, LANES), 0)
    start = 8 * (3 - lax.axis_index("y"))
    nothing_before = (row >= start) & (row < start + 2)
    upper = row % 4 >= 2
    quarters = [[ref[pl.ds((4 * tile + g) * 8, 8), :] for ref in blocks] for g in range(4)]
    codes = []
    for slot in range(4):
        code = list(quarters[-slot % 4])
        for group in range(1, 4):
            source = quarters[(group - slot) % 4]
            code = [jnp.where(lane_group == group, source[i], code[i]) for i in range(4)]
        code = jnp.concatenate([piece.astype(jnp.float32) for piece in code], axis=0)
        codes.append(pltpu.roll(code, LANES - slot * IN_BLK, 1) if slot else code)
    shift = jnp.where(upper, codes[3], pltpu.roll(codes[3], rows - 2, 0))
    values = []
    for slot in range(4):
        value = jnp.exp2(jnp.log2(jnp.abs(codes[slot])) * (1.0 / POWER) + shift)
        value = jnp.where(codes[slot] < 0.0, -value, value)
        if slot < TAPS - 1:
            value = value + jnp.where(nothing_before, 0.0, pltpu.roll(value, 2, 0))
        values.append(value)
    pairs = [jnp.where(upper, pltpu.roll(values[i + 1], 2, 0), values[i]) for i in (0, 2)]
    return jnp.concatenate(pairs, axis=0)


def gram_kernel(b0_ref, b1_ref, b2_ref, b3_ref, out_hbm, vis_ref, sems):
    blocks = (b0_ref, b1_ref, b2_ref, b3_ref)
    left = frames_of(blocks, 2 * lax.axis_index("y") + lax.axis_index("zh")) * (1.0 / (FRQ * FR_BLK))
    real = lax.broadcasted_iota(jnp.int32, left.shape, 0) % 2 == 0
    turned = jnp.where(real, pltpu.roll(left, left.shape[0] - 1, 0), -pltpu.roll(left, 1, 0))
    high, low = two_terms(jnp.concatenate([left, turned], axis=1))
    left = jnp.concatenate([high, high, low], axis=0)
    row = lax.broadcasted_iota(jnp.int32, (2 * LANES, 2 * LANES), 0)
    col = lax.broadcasted_iota(jnp.int32, (2 * LANES, 2 * LANES), 1)
    order = jnp.where(col == row % 2 * LANES + row // 2, 1.0, 0.0).astype(jnp.bfloat16)
    left = lax.dot_general(order, left, (((1,), (1,)), ((), ())), preferred_element_type=jnp.float32)
    left = left.astype(jnp.bfloat16)
    copies = []
    for pair in range(4):
        high, low = two_terms(jnp.concatenate([frames_of(blocks, 2 * pair + i) for i in range(2)], axis=1))
        right = jnp.concatenate([high, low, high], axis=0)
        vis = jnp.dot(left, right, preferred_element_type=jnp.float32)
        for i in range(2):
            tile = 2 * pair + i
            vis_ref.at[tile].reshape(2 * LANES, LANES)[...] = vis[:, i * LANES : (i + 1) * LANES]
            copies.append(pltpu.make_async_copy(vis_ref.at[tile], out_hbm.at[:, tile], sems.at[tile]))
            copies[-1].start()
    for copy in copies:
        copy.wait()


def body(voltages, history, window):
    vmem = pl.BlockSpec(memory_space=pltpu.VMEM)
    hbm = pl.BlockSpec(memory_space=pl.ANY)
    past = history.transpose(1, 0, 2).reshape((TAPS - 1) * IN_BLK, SAMPLES)
    chunks = pl.pallas_call(
        transform_kernel,
        out_shape=pltpu.VMEM((2 * LANES, LANES), jnp.bfloat16),
        in_specs=[hbm] * 4,
        out_specs=vmem,
        scratch_shapes=[
            pltpu.VMEM((SAMPLES // LANES, IN_BLK, FR_BLK, LANES), jnp.bfloat16),
            pltpu.VMEM(past.shape, jnp.bfloat16),
            pltpu.VMEM(window.shape, jnp.float32),
            pltpu.VMEM((2 * CHANNELS, SAMPLES), jnp.float32),
            pltpu.VMEM((2 * LANES, LANES), jnp.float32),
            pltpu.VMEM((2 * CHANNELS, LANES), jnp.float32),
            pltpu.SemaphoreType.DMA((4,)),
        ],
        name="transform",
    )(voltages, past, window, jnp.asarray(dft_table()))
    chunks = chunks.reshape(2 * CHANNELS, 4, LANES)
    mine = lax.all_to_all(chunks, ("x", "zl", "c", "zh"), 0, 0, tiled=True).reshape(2 * LANES, LANES)
    ahead, behind, across = (lax.ppermute(mine, "y", [(i, (i + k) % 4) for i in range(4)]) for k in (1, 3, 2))
    blocks = [pltpu.with_memory_space_constraint(x, pltpu.VMEM) for x in (behind, across, ahead, mine)]
    tiles = pl.pallas_call(
        gram_kernel,
        out_shape=jax.ShapeDtypeStruct((LANES, 8, 2, LANES), jnp.float32),
        in_specs=[vmem] * 4,
        out_specs=hbm,
        scratch_shapes=[pltpu.VMEM((8, LANES, 2, LANES), jnp.float32), pltpu.SemaphoreType.DMA((8,))],
        name="gram",
    )(*blocks)
    return tiles.transpose(0, 2, 1, 3).reshape(LANES, 1, 2, 8 * LANES)


def solution(mesh):
    fine = jax.sharding.Mesh(mesh.devices.reshape(4, 4, 2, 4, 2), ("x", "zl", "c", "y", "zh"))
    inp, frq = ("x", "zl", "c"), ("y", "zh")
    return jax.shard_map(
        body,
        mesh=fine,
        in_specs=(P(inp, frq, None), P(inp, None, None), P()),
        out_specs=P(frq, inp, None, None),
        check_vma=False,
    )
```

```python
import math

import jax
import jax.numpy as jnp
import numpy as np
from jax import lax
from jax.experimental import pallas as pl
from jax.experimental.pallas import tpu as pltpu
from jax.sharding import PartitionSpec as P

TAPS = 4
SAMPLES = 2048
CHANNELS = 32
CHAN_FIRST = 496
IN_BLK = 32
FR_BLK = 4
FRQ = 8
LANES = 128
STEP = 256
POWER = 16
TOP = 7


def dft_start():
    bins = np.arange(CHANNELS, dtype=np.int64) + CHAN_FIRST
    turns = bins[:, None] * np.arange(LANES, dtype=np.int64)[None, :] % SAMPLES
    begin = np.exp(turns * (-2j * math.pi / SAMPLES)) / math.sqrt(SAMPLES)
    turn = np.exp(bins[:, None] * LANES % SAMPLES * (-2j * math.pi / SAMPLES)) * np.ones((1, LANES))
    return np.concatenate([begin.real, begin.imag, turn.real, turn.imag]).astype(np.float32)


def two_terms(x):
    high = x.astype(jnp.bfloat16)
    low = (x - high.astype(jnp.float32)).astype(jnp.bfloat16)
    return high, low


def products(start_ref, window_ref, taps, frames_at):
    dims = (((1,), (1,)), ((), ()))
    total = None
    real, imag, turn_real, turn_imag = (start_ref[part * CHANNELS : (part + 1) * CHANNELS, :] for part in range(4))
    for step in range(SAMPLES // STEP):
        cols = slice(step * STEP, (step + 1) * STEP)
        table = []
        for _ in range(STEP // LANES):
            table.append(jnp.concatenate([real, imag], axis=0))
            real, imag = real * turn_real - imag * turn_imag, real * turn_imag + imag * turn_real
        table = jnp.concatenate(table, axis=1)
        weights = jnp.concatenate([table * window_ref[tap : tap + 1, cols] for tap in range(taps)], axis=0)
        high, low = two_terms(weights)
        frames = frames_at(step)
        part = lax.dot_general(high, frames, dims, preferred_element_type=jnp.float32)
        part = part + lax.dot_general(low, frames, dims, preferred_element_type=jnp.float32)
        total = part if total is None else total + part
    return [total[tap * 2 * CHANNELS : (tap + 1) * 2 * CHANNELS] for tap in range(taps)]


def transform_kernel(volt_hbm, hist_hbm, window_hbm, start_hbm, out_ref,
                     volt_ref, hist_ref, window_ref, start_ref, rows_ref, past_ref, sems):
    first = (lax.axis_index("y") == 0) & (lax.axis_index("zh") == 0)
    hist_copy = pltpu.make_async_copy(hist_hbm, hist_ref, sems.at[3])
    pltpu.make_async_copy(window_hbm, window_ref, sems.at[0]).start()
    pltpu.make_async_copy(start_hbm, start_ref, sems.at[1]).start()
    for tile in range(SAMPLES // LANES):
        pltpu.make_async_copy(volt_hbm.at[:, :, pl.ds(tile * LANES, LANES)], volt_ref.at[tile], sems.at[2]).start()
    lane = lax.broadcasted_iota(jnp.int32, (2 * CHANNELS, LANES), 1)
    past_ref[...] = jnp.zeros((2 * CHANNELS, LANES), jnp.float32)
    pltpu.make_async_copy(window_hbm, window_ref, sems.at[0]).wait()
    pltpu.make_async_copy(start_hbm, start_ref, sems.at[1]).wait()

    @pl.when(first)
    def _():
        hist_copy.start()
        hist_copy.wait()

        def frames_at(step):
            rows = hist_ref[:, step * STEP : (step + 1) * STEP]
            return jnp.concatenate([rows, jnp.zeros((IN_BLK, STEP), jnp.bfloat16)], axis=0)

        past = jnp.zeros((2 * CHANNELS, LANES), jnp.float32)
        for tap, before in enumerate(products(start_ref, window_ref, TAPS - 1, frames_at)):
            if tap:
                before = pltpu.roll(before, LANES - tap * IN_BLK, 1)
            past = past + jnp.where(lane < (TAPS - 1 - tap) * IN_BLK, before, 0.0)
        past_ref[...] = past

    pltpu.make_async_copy(volt_ref, volt_ref, sems.at[2]).wait()

    def frames_at(step):
        tiles = range(step * STEP // LANES, (step + 1) * STEP // LANES)
        return jnp.concatenate([volt_ref.at[tile].reshape(LANES, LANES)[...] for tile in tiles], axis=1)

    frame = lane % FR_BLK
    own = later = None
    for tap, here in enumerate(products(start_ref, window_ref, TAPS, frames_at)):
        moved = TAPS - 1 - tap
        if moved == 0:
            own = own + here
            continue
        kept = jnp.where(frame < moved, 0.0, pltpu.roll(here, moved, 1))
        passed = jnp.where(frame < moved, pltpu.roll(here, LANES - FR_BLK + moved, 1), 0.0)
        own = kept if own is None else own + kept
        later = passed if later is None else later + passed
    last = (lax.axis_index("y") == 3) & (lax.axis_index("zh") == 1)
    later = jnp.where(last, 0.0, later)
    past = past_ref[...]
    top = jnp.maximum(jnp.maximum(jnp.abs(own), jnp.abs(later)), jnp.abs(past))
    top = jnp.maximum(top[:CHANNELS], top[CHANNELS:])
    top = jnp.maximum(jnp.max(top, axis=1, keepdims=True), 2.0**-100)
    shift = jnp.broadcast_to(jnp.ceil(jnp.log2(top)) - (TOP - 1), (CHANNELS, LANES))
    factor = jnp.exp2(-shift)
    row = lax.broadcasted_iota(jnp.int32, (LANES, LANES), 0)
    col = lax.broadcasted_iota(jnp.int32, (LANES, LANES), 1)
    order = jnp.where(col == row % FR_BLK * IN_BLK + row // FR_BLK, 1.0, 0.0).astype(jnp.bfloat16)
    high, low = two_terms(jnp.concatenate([own, later], axis=0))
    sorted_rows = jnp.dot(high, order, preferred_element_type=jnp.float32)
    sorted_rows = sorted_rows + jnp.dot(low, order, preferred_element_type=jnp.float32)
    own = sorted_rows[: 2 * CHANNELS] + past
    later = sorted_rows[2 * CHANNELS :]
    quads = [own[:CHANNELS], own[CHANNELS:], later[:CHANNELS], later[CHANNELS:]]
    lane = lane[:CHANNELS]
    for kind in range(4):
        value = quads[kind] * factor
        power = value * value
        power = power * power
        power = power * power
        power = power * power
        value = jnp.where(value < 0.0, -power, power)
        if kind >= 2:
            value = jnp.where(lane < (TAPS - 1) * IN_BLK, value, shift)
        value = pltpu.roll(value, (lax.axis_index("zl") % 2 * 2 + lax.axis_index("c")) * IN_BLK, 1)
        for copy in range(2):
            rows_ref[pl.ds(4 * copy + kind, CHANNELS, 8), :] = value
    out_ref[...] = rows_ref[...].astype(jnp.bfloat16)


def decode_kernel(got_ref, sums_ref, passed_ref):
    lane_group = lax.broadcasted_iota(jnp.int32, (8, LANES), 1) // IN_BLK
    row = lax.broadcasted_iota(jnp.int32, (8, LANES), 0)
    upper = row % 4 >= 2
    for tile in range(8):
        quarters = [got_ref[pl.ds((4 * tile + g) * 8, 8), :].astype(jnp.float32) for g in range(4)]
        halves = [jnp.where(lane_group < 2, quarters[-slot % 4], quarters[(2 - slot) % 4]) for slot in range(4)]
        codes = [jnp.where(lane_group % 2 == 0, halves[slot], halves[slot - 1]) for slot in range(4)]
        codes = [pltpu.roll(code, (-slot % 4) * IN_BLK, 1) if slot else code for slot, code in enumerate(codes)]
        shift = jnp.where(upper, codes[3], pltpu.roll(codes[3], 6, 0))
        values = []
        moved = []
        for code in codes:
            size = jnp.maximum(jnp.abs(code), 2.0**-126)
            values.append(code * jnp.exp2(jnp.log2(size) * (1.0 / POWER - 1.0) + shift))
        for slot in range(TAPS - 1):
            moved.append(pltpu.roll(values[slot], 2, 0))
            values[slot] = values[slot] + jnp.where(row >= 4, moved[slot], 0.0)
        for pair in range(2):
            rows = pl.ds(8 * pair, 8)
            sums_ref[tile, rows, :] = jnp.where(upper, pltpu.roll(values[2 * pair + 1], 2, 0), values[2 * pair])
        second = jnp.where(row < 4, pltpu.roll(moved[1], 2, 0), 0.0)
        passed_ref[tile, :8, :] = jnp.where(row < 2, moved[0], second)
        passed_ref[tile, 8:, :] = jnp.where(row < 2, moved[2], 0.0)


def gram_kernel(*refs):
    sums_refs, passed_refs, out_hbm, vis_ref, sems = refs[:4], refs[4:8], *refs[8:]

    def frames_of(tile):
        return jnp.concatenate([sums_refs[i][tile] + passed_refs[i - 1][tile] for i in range(4)], axis=0)

    tile = 2 * lax.axis_index("y") + lax.axis_index("zh")
    left = frames_of(tile) * (1.0 / (FRQ * FR_BLK))
    real = lax.broadcasted_iota(jnp.int32, left.shape, 0) % 2 == 0
    turned = jnp.where(real, pltpu.roll(left, left.shape[0] - 1, 0), -pltpu.roll(left, 1, 0))
    high, low = two_terms(jnp.concatenate([left, turned], axis=1))
    left = jnp.concatenate([high, high, low], axis=0)
    row = lax.broadcasted_iota(jnp.int32, (2 * LANES, 2 * LANES), 0)
    col = lax.broadcasted_iota(jnp.int32, (2 * LANES, 2 * LANES), 1)
    order = jnp.where(col == row % 2 * LANES + row // 2, 1.0, 0.0).astype(jnp.bfloat16)
    left = lax.dot_general(order, left, (((1,), (1,)), ((), ())), preferred_element_type=jnp.float32)
    left = left.astype(jnp.bfloat16)
    copies = []
    for pair in range(4):
        high, low = two_terms(jnp.concatenate([frames_of(2 * pair + i) for i in range(2)], axis=1))
        right = jnp.concatenate([high, low, high], axis=0)
        vis = jnp.dot(left, right, preferred_element_type=jnp.float32)
        for i in range(2):
            tile = 2 * pair + i
            vis_ref.at[tile].reshape(2 * LANES, LANES)[...] = vis[:, i * LANES : (i + 1) * LANES]
            copies.append(pltpu.make_async_copy(vis_ref.at[tile], out_hbm.at[:, tile], sems.at[tile]))
            copies[-1].start()
    for copy in copies:
        copy.wait()


def body(voltages, history, window):
    vmem = pl.BlockSpec(memory_space=pltpu.VMEM)
    hbm = pl.BlockSpec(memory_space=pl.ANY)
    past = history.transpose(1, 0, 2).reshape((TAPS - 1) * IN_BLK, SAMPLES)
    chunks = pl.pallas_call(
        transform_kernel,
        out_shape=pltpu.VMEM((2 * LANES, LANES), jnp.bfloat16),
        in_specs=[hbm] * 4,
        out_specs=vmem,
        scratch_shapes=[
            pltpu.VMEM((SAMPLES // LANES, IN_BLK, FR_BLK, LANES), jnp.bfloat16),
            pltpu.VMEM(past.shape, jnp.bfloat16),
            pltpu.VMEM(window.shape, jnp.float32),
            pltpu.VMEM((4 * CHANNELS, LANES), jnp.float32),
            pltpu.VMEM((2 * LANES, LANES), jnp.float32),
            pltpu.VMEM((2 * CHANNELS, LANES), jnp.float32),
            pltpu.SemaphoreType.DMA((4,)),
        ],
        name="transform",
    )(voltages, past, window, jnp.asarray(dft_start()))
    chunks = chunks.reshape(2 * CHANNELS, 4, LANES)
    mine = lax.all_to_all(chunks, ("x", "zl", "c", "zh"), 0, 0, tiled=True).reshape(2 * LANES, LANES)
    ahead, behind, across = (lax.ppermute(mine, "y", [(i, (i + k) % 4) for i in range(4)]) for k in (1, 3, 2))
    sums, passed = [], []
    for i, piece in enumerate((behind, across, ahead, mine)):
        found = pl.pallas_call(
            decode_kernel,
            out_shape=[pltpu.VMEM((8, 2 * 8, LANES), jnp.float32)] * 2,
            in_specs=[vmem],
            out_specs=[vmem] * 2,
            name=f"decode{i}",
        )(pltpu.with_memory_space_constraint(piece, pltpu.VMEM))
        sums.append(pltpu.with_memory_space_constraint(found[0], pltpu.VMEM))
        passed.append(pltpu.with_memory_space_constraint(found[1], pltpu.VMEM))
    tiles = pl.pallas_call(
        gram_kernel,
        out_shape=jax.ShapeDtypeStruct((LANES, 8, 2, LANES), jnp.float32),
        in_specs=[vmem] * 8,
        out_specs=hbm,
        scratch_shapes=[pltpu.VMEM((8, LANES, 2, LANES), jnp.float32), pltpu.SemaphoreType.DMA((8,))],
        name="gram",
    )(*sums, *passed)
    return tiles.transpose(0, 2, 1, 3).reshape(LANES, 1, 2, 8 * LANES)


def solution(mesh):
    fine = jax.sharding.Mesh(mesh.devices.reshape(4, 4, 2, 4, 2), ("x", "zl", "c", "y", "zh"))
    inp, frq = ("x", "zl", "c"), ("y", "zh")
    return jax.shard_map(
        body,
        mesh=fine,
        in_specs=(P(inp, frq, None), P(inp, None, None), P()),
        out_specs=P(frq, inp, None, None),
        check_vma=False,
    )
```

```python
import math

import jax
import jax.numpy as jnp
import numpy as np
from jax import lax
from jax.experimental import pallas as pl
from jax.experimental.pallas import tpu as pltpu
from jax.sharding import PartitionSpec as P

TAPS = 4
SAMPLES = 2048
CHANNELS = 32
CHAN_FIRST = 496
IN_BLK = 32
FR_BLK = 4
FRQ = 8
LANES = 128
STEP = 256
POWER = 16
TOP = 7


def dft_start():
    bins = np.arange(CHANNELS, dtype=np.int64) + CHAN_FIRST
    turns = bins[:, None] * np.arange(LANES, dtype=np.int64)[None, :] % SAMPLES
    begin = np.exp(turns * (-2j * math.pi / SAMPLES)) / math.sqrt(SAMPLES)
    turn = np.exp(bins[:, None] * LANES % SAMPLES * (-2j * math.pi / SAMPLES)) * np.ones((1, LANES))
    return np.concatenate([begin.real, begin.imag, turn.real, turn.imag]).astype(np.float32)


def two_terms(x):
    high = x.astype(jnp.bfloat16)
    low = (x - high.astype(jnp.float32)).astype(jnp.bfloat16)
    return high, low


def products(start_ref, window_ref, taps, frames_at):
    dims = (((1,), (1,)), ((), ()))
    total = None
    real, imag, turn_real, turn_imag = (start_ref[part * CHANNELS : (part + 1) * CHANNELS, :] for part in range(4))
    for step in range(SAMPLES // STEP):
        cols = slice(step * STEP, (step + 1) * STEP)
        table = []
        for _ in range(STEP // LANES):
            table.append(jnp.concatenate([real, imag], axis=0))
            real, imag = real * turn_real - imag * turn_imag, real * turn_imag + imag * turn_real
        table = jnp.concatenate(table, axis=1)
        weights = jnp.concatenate([table * window_ref[tap : tap + 1, cols] for tap in range(taps)], axis=0)
        high, low = two_terms(weights)
        frames = frames_at(step)
        part = lax.dot_general(high, frames, dims, preferred_element_type=jnp.float32)
        part = part + lax.dot_general(low, frames, dims, preferred_element_type=jnp.float32)
        total = part if total is None else total + part
    return [total[tap * 2 * CHANNELS : (tap + 1) * 2 * CHANNELS] for tap in range(taps)]


def transform_kernel(volt_hbm, hist_hbm, window_hbm, start_hbm, out_ref,
                     volt_ref, hist_ref, window_ref, start_ref, rows_ref, past_ref, sems):
    first = (lax.axis_index("y") == 0) & (lax.axis_index("zh") == 0)
    hist_copy = pltpu.make_async_copy(hist_hbm, hist_ref, sems.at[3])
    pltpu.make_async_copy(window_hbm, window_ref, sems.at[0]).start()
    pltpu.make_async_copy(start_hbm, start_ref, sems.at[1]).start()
    for tile in range(SAMPLES // LANES):
        pltpu.make_async_copy(volt_hbm.at[:, :, pl.ds(tile * LANES, LANES)], volt_ref.at[tile], sems.at[2]).start()

    @pl.when(first)
    def _():
        hist_copy.start()

    lane = lax.broadcasted_iota(jnp.int32, (2 * CHANNELS, LANES), 1)
    past_ref[...] = jnp.zeros((2 * CHANNELS, LANES), jnp.float32)
    pltpu.make_async_copy(window_hbm, window_ref, sems.at[0]).wait()
    pltpu.make_async_copy(start_hbm, start_ref, sems.at[1]).wait()

    @pl.when(first)
    def _():
        hist_copy.wait()

        def frames_at(step):
            rows = hist_ref[:, step * STEP : (step + 1) * STEP]
            return jnp.concatenate([rows, jnp.zeros((IN_BLK, STEP), jnp.bfloat16)], axis=0)

        past = jnp.zeros((2 * CHANNELS, LANES), jnp.float32)
        for tap, before in enumerate(products(start_ref, window_ref, TAPS - 1, frames_at)):
            if tap:
                before = pltpu.roll(before, LANES - tap * IN_BLK, 1)
            past = past + jnp.where(lane < (TAPS - 1 - tap) * IN_BLK, before, 0.0)
        past_ref[...] = past

    pltpu.make_async_copy(volt_ref, volt_ref, sems.at[2]).wait()

    def frames_at(step):
        tiles = range(step * STEP // LANES, (step + 1) * STEP // LANES)
        return jnp.concatenate([volt_ref.at[tile].reshape(LANES, LANES)[...] for tile in tiles], axis=1)

    frame = lane % FR_BLK
    own = later = None
    for tap, here in enumerate(products(start_ref, window_ref, TAPS, frames_at)):
        moved = TAPS - 1 - tap
        if moved == 0:
            own = own + here
            continue
        kept = jnp.where(frame < moved, 0.0, pltpu.roll(here, moved, 1))
        passed = jnp.where(frame < moved, pltpu.roll(here, LANES - FR_BLK + moved, 1), 0.0)
        own = kept if own is None else own + kept
        later = passed if later is None else later + passed
    last = (lax.axis_index("y") == 3) & (lax.axis_index("zh") == 1)
    later = jnp.where(last, 0.0, later)
    past = past_ref[...]
    top = jnp.maximum(jnp.maximum(jnp.abs(own), jnp.abs(later)), jnp.abs(past))
    top = jnp.maximum(top[:CHANNELS], top[CHANNELS:])
    top = jnp.maximum(jnp.max(top, axis=1, keepdims=True), 2.0**-100)
    shift = jnp.broadcast_to(jnp.ceil(jnp.log2(top)) - (TOP - 1), (CHANNELS, LANES))
    factor = jnp.exp2(-shift)
    row = lax.broadcasted_iota(jnp.int32, (LANES, LANES), 0)
    col = lax.broadcasted_iota(jnp.int32, (LANES, LANES), 1)
    order = jnp.where(col == row % FR_BLK * IN_BLK + row // FR_BLK, 1.0, 0.0).astype(jnp.bfloat16)
    high, low = two_terms(jnp.concatenate([own, later], axis=0))
    sorted_rows = jnp.dot(high, order, preferred_element_type=jnp.float32)
    sorted_rows = sorted_rows + jnp.dot(low, order, preferred_element_type=jnp.float32)
    own = sorted_rows[: 2 * CHANNELS] + past
    later = sorted_rows[2 * CHANNELS :]
    quads = [own[:CHANNELS], own[CHANNELS:], later[:CHANNELS], later[CHANNELS:]]
    lane = lane[:CHANNELS]
    for kind in range(4):
        value = quads[kind] * factor
        power = value * value
        power = power * power
        power = power * power
        power = power * power
        value = jnp.where(value < 0.0, -power, power)
        if kind >= 2:
            value = jnp.where(lane < (TAPS - 1) * IN_BLK, value, shift)
        value = pltpu.roll(value, (lax.axis_index("zl") % 2 * 2 + lax.axis_index("c")) * IN_BLK, 1)
        for copy in range(2):
            rows_ref[pl.ds(4 * copy + kind, CHANNELS, 8), :] = value
    out_ref[...] = rows_ref[...].astype(jnp.bfloat16)


def decode_kernel(got_ref, sums_ref, passed_ref):
    lane_group = lax.broadcasted_iota(jnp.int32, (8, LANES), 1) // IN_BLK
    row = lax.broadcasted_iota(jnp.int32, (8, LANES), 0)
    upper = row % 4 >= 2
    for tile in range(8):
        quarters = [got_ref[pl.ds((4 * tile + g) * 8, 8), :].astype(jnp.float32) for g in range(4)]
        halves = [jnp.where(lane_group < 2, quarters[-slot % 4], quarters[(2 - slot) % 4]) for slot in range(4)]
        codes = [jnp.where(lane_group % 2 == 0, halves[slot], halves[slot - 1]) for slot in range(4)]
        codes = [pltpu.roll(code, (-slot % 4) * IN_BLK, 1) if slot else code for slot, code in enumerate(codes)]
        shift = jnp.where(upper, codes[3], pltpu.roll(codes[3], 6, 0))
        values = []
        moved = []
        for code in codes:
            size = jnp.maximum(jnp.abs(code), 2.0**-126)
            values.append(code * jnp.exp2(jnp.log2(size) * (1.0 / POWER - 1.0) + shift))
        for slot in range(TAPS - 1):
            moved.append(pltpu.roll(values[slot], 2, 0))
            values[slot] = values[slot] + jnp.where(row >= 4, moved[slot], 0.0)
        for pair in range(2):
            rows = pl.ds(8 * pair, 8)
            sums_ref[tile, rows, :] = jnp.where(upper, pltpu.roll(values[2 * pair + 1], 2, 0), values[2 * pair])
        second = jnp.where(row < 4, pltpu.roll(moved[1], 2, 0), 0.0)
        passed_ref[tile, :8, :] = jnp.where(row < 2, moved[0], second)
        passed_ref[tile, 8:, :] = jnp.where(row < 2, moved[2], 0.0)


def gram_kernel(*refs):
    sums_refs, passed_refs, out_hbm, vis_ref, sems = refs[:4], refs[4:8], *refs[8:]

    def frames_of(tile):
        return jnp.concatenate([sums_refs[i][tile] + passed_refs[i - 1][tile] for i in range(4)], axis=0)

    tile = 2 * lax.axis_index("y") + lax.axis_index("zh")
    left = frames_of(tile) * (1.0 / (FRQ * FR_BLK))
    real = lax.broadcasted_iota(jnp.int32, left.shape, 0) % 2 == 0
    turned = jnp.where(real, pltpu.roll(left, left.shape[0] - 1, 0), -pltpu.roll(left, 1, 0))
    high, low = two_terms(jnp.concatenate([left, turned], axis=1))
    left = jnp.concatenate([high, high, low], axis=0)
    row = lax.broadcasted_iota(jnp.int32, (2 * LANES, 2 * LANES), 0)
    col = lax.broadcasted_iota(jnp.int32, (2 * LANES, 2 * LANES), 1)
    order = jnp.where(col == row % 2 * LANES + row // 2, 1.0, 0.0).astype(jnp.bfloat16)
    left = lax.dot_general(order, left, (((1,), (1,)), ((), ())), preferred_element_type=jnp.float32)
    left = left.astype(jnp.bfloat16)
    copies = []
    for pair in range(4):
        high, low = two_terms(jnp.concatenate([frames_of(2 * pair + i) for i in range(2)], axis=1))
        right = jnp.concatenate([high, low, high], axis=0)
        vis = jnp.dot(left, right, preferred_element_type=jnp.float32)
        for i in range(2):
            tile = 2 * pair + i
            vis_ref.at[tile].reshape(2 * LANES, LANES)[...] = vis[:, i * LANES : (i + 1) * LANES]
            copies.append(pltpu.make_async_copy(vis_ref.at[tile], out_hbm.at[:, tile], sems.at[tile]))
            copies[-1].start()
    for copy in copies:
        copy.wait()


def body(voltages, history, window):
    vmem = pl.BlockSpec(memory_space=pltpu.VMEM)
    hbm = pl.BlockSpec(memory_space=pl.ANY)
    past = history.transpose(1, 0, 2).reshape((TAPS - 1) * IN_BLK, SAMPLES)
    chunks = pl.pallas_call(
        transform_kernel,
        out_shape=pltpu.VMEM((2 * LANES, LANES), jnp.bfloat16),
        in_specs=[hbm] * 4,
        out_specs=vmem,
        scratch_shapes=[
            pltpu.VMEM((SAMPLES // LANES, IN_BLK, FR_BLK, LANES), jnp.bfloat16),
            pltpu.VMEM(past.shape, jnp.bfloat16),
            pltpu.VMEM(window.shape, jnp.float32),
            pltpu.VMEM((4 * CHANNELS, LANES), jnp.float32),
            pltpu.VMEM((2 * LANES, LANES), jnp.float32),
            pltpu.VMEM((2 * CHANNELS, LANES), jnp.float32),
            pltpu.SemaphoreType.DMA((4,)),
        ],
        name="transform",
    )(voltages, past, window, jnp.asarray(dft_start()))
    chunks = chunks.reshape(2 * CHANNELS, 4, LANES)
    mine = lax.all_to_all(chunks, ("x", "zl", "c", "zh"), 0, 0, tiled=True).reshape(2 * LANES, LANES)
    ahead, behind, across = (lax.ppermute(mine, "y", [(i, (i + k) % 4) for i in range(4)]) for k in (1, 3, 2))
    sums, passed = [], []
    for i, piece in enumerate((behind, across, ahead, mine)):
        found = pl.pallas_call(
            decode_kernel,
            out_shape=[pltpu.VMEM((8, 2 * 8, LANES), jnp.float32)] * 2,
            in_specs=[vmem],
            out_specs=[vmem] * 2,
            name=f"decode{i}",
        )(pltpu.with_memory_space_constraint(piece, pltpu.VMEM))
        sums.append(pltpu.with_memory_space_constraint(found[0], pltpu.VMEM))
        passed.append(pltpu.with_memory_space_constraint(found[1], pltpu.VMEM))
    tiles = pl.pallas_call(
        gram_kernel,
        out_shape=jax.ShapeDtypeStruct((LANES, 8, 2, LANES), jnp.float32),
        in_specs=[vmem] * 8,
        out_specs=hbm,
        scratch_shapes=[pltpu.VMEM((8, LANES, 2, LANES), jnp.float32), pltpu.SemaphoreType.DMA((8,))],
        name="gram",
    )(*sums, *passed)
    return tiles.transpose(0, 2, 1, 3).reshape(LANES, 1, 2, 8 * LANES)


def solution(mesh):
    fine = jax.sharding.Mesh(mesh.devices.reshape(4, 4, 2, 4, 2), ("x", "zl", "c", "y", "zh"))
    inp, frq = ("x", "zl", "c"), ("y", "zh")
    return jax.shard_map(
        body,
        mesh=fine,
        in_specs=(P(inp, frq, None), P(inp, None, None), P()),
        out_specs=P(frq, inp, None, None),
        check_vma=False,
    )
```

```python
import math

import jax
import jax.numpy as jnp
import numpy as np
from jax import lax
from jax.experimental import pallas as pl
from jax.experimental.pallas import tpu as pltpu
from jax.sharding import PartitionSpec as P

TAPS = 4
SAMPLES = 2048
CHANNELS = 32
CHAN_FIRST = 496
IN_BLK = 32
FR_BLK = 4
FRQ = 8
LANES = 128
STEP = 256
POWER = 16
TOP = 7


def dft_start():
    bins = np.arange(CHANNELS, dtype=np.int64) + CHAN_FIRST
    turns = bins[:, None] * np.arange(LANES, dtype=np.int64)[None, :] % SAMPLES
    begin = np.exp(turns * (-2j * math.pi / SAMPLES)) / math.sqrt(SAMPLES)
    turn = np.exp(bins[:, None] * LANES % SAMPLES * (-2j * math.pi / SAMPLES)) * np.ones((1, LANES))
    return np.concatenate([begin.real, begin.imag, turn.real, turn.imag]).astype(np.float32)


def two_terms(x):
    high = x.astype(jnp.bfloat16)
    low = (x - high.astype(jnp.float32)).astype(jnp.bfloat16)
    return high, low


def products(start_ref, window_ref, taps, frames_at):
    dims = (((1,), (1,)), ((), ()))
    total = None
    real, imag, turn_real, turn_imag = (start_ref[part * CHANNELS : (part + 1) * CHANNELS, :] for part in range(4))
    for step in range(SAMPLES // STEP):
        cols = slice(step * STEP, (step + 1) * STEP)
        table = []
        for _ in range(STEP // LANES):
            table.append(jnp.concatenate([real, imag], axis=0))
            real, imag = real * turn_real - imag * turn_imag, real * turn_imag + imag * turn_real
        table = jnp.concatenate(table, axis=1)
        weights = jnp.concatenate([table * window_ref[tap : tap + 1, cols] for tap in range(taps)], axis=0)
        high, low = two_terms(weights)
        frames = frames_at(step)
        part = lax.dot_general(jnp.concatenate([high, low], axis=0), frames, dims, preferred_element_type=jnp.float32)
        total = part if total is None else total + part
    total = total[: total.shape[0] // 2] + total[total.shape[0] // 2 :]
    return [total[tap * 2 * CHANNELS : (tap + 1) * 2 * CHANNELS] for tap in range(taps)]


def transform_kernel(volt_hbm, hist_hbm, window_hbm, start_hbm, out_ref,
                     volt_ref, hist_ref, window_ref, start_ref, rows_ref, past_ref, sems):
    first = (lax.axis_index("y") == 0) & (lax.axis_index("zh") == 0)
    hist_copy = pltpu.make_async_copy(hist_hbm, hist_ref, sems.at[3])
    pltpu.make_async_copy(window_hbm, window_ref, sems.at[0]).start()
    pltpu.make_async_copy(start_hbm, start_ref, sems.at[1]).start()
    for tile in range(SAMPLES // LANES):
        pltpu.make_async_copy(volt_hbm.at[:, :, pl.ds(tile * LANES, LANES)], volt_ref.at[tile], sems.at[2]).start()

    @pl.when(first)
    def _():
        hist_copy.start()

    lane = lax.broadcasted_iota(jnp.int32, (2 * CHANNELS, LANES), 1)
    past_ref[...] = jnp.zeros((2 * CHANNELS, LANES), jnp.float32)
    pltpu.make_async_copy(window_hbm, window_ref, sems.at[0]).wait()
    pltpu.make_async_copy(start_hbm, start_ref, sems.at[1]).wait()

    @pl.when(first)
    def _():
        hist_copy.wait()

        def frames_at(step):
            rows = hist_ref[:, step * STEP : (step + 1) * STEP]
            return jnp.concatenate([rows, jnp.zeros((IN_BLK, STEP), jnp.bfloat16)], axis=0)

        past = jnp.zeros((2 * CHANNELS, LANES), jnp.float32)
        for tap, before in enumerate(products(start_ref, window_ref, TAPS - 1, frames_at)):
            if tap:
                before = pltpu.roll(before, LANES - tap * IN_BLK, 1)
            past = past + jnp.where(lane < (TAPS - 1 - tap) * IN_BLK, before, 0.0)
        past_ref[...] = past

    pltpu.make_async_copy(volt_ref, volt_ref, sems.at[2]).wait()

    def frames_at(step):
        tiles = range(step * STEP // LANES, (step + 1) * STEP // LANES)
        return jnp.concatenate([volt_ref.at[tile].reshape(LANES, LANES)[...] for tile in tiles], axis=1)

    frame = lane % FR_BLK
    own = later = None
    for tap, here in enumerate(products(start_ref, window_ref, TAPS, frames_at)):
        moved = TAPS - 1 - tap
        if moved == 0:
            own = own + here
            continue
        kept = jnp.where(frame < moved, 0.0, pltpu.roll(here, moved, 1))
        passed = jnp.where(frame < moved, pltpu.roll(here, LANES - FR_BLK + moved, 1), 0.0)
        own = kept if own is None else own + kept
        later = passed if later is None else later + passed
    last = (lax.axis_index("y") == 3) & (lax.axis_index("zh") == 1)
    later = jnp.where(last, 0.0, later)
    past = past_ref[...]
    top = jnp.maximum(jnp.maximum(jnp.abs(own), jnp.abs(later)), jnp.abs(past))
    top = jnp.maximum(top[:CHANNELS], top[CHANNELS:])
    top = jnp.maximum(jnp.max(top, axis=1, keepdims=True), 2.0**-100)
    shift = jnp.broadcast_to(jnp.ceil(jnp.log2(top)) - (TOP - 1), (CHANNELS, LANES))
    factor = jnp.exp2(-shift)
    row = lax.broadcasted_iota(jnp.int32, (LANES, LANES), 0)
    col = lax.broadcasted_iota(jnp.int32, (LANES, LANES), 1)
    order = jnp.where(col == row % FR_BLK * IN_BLK + row // FR_BLK, 1.0, 0.0).astype(jnp.bfloat16)
    high, low = two_terms(jnp.concatenate([own, later], axis=0))
    sorted_rows = jnp.dot(high, order, preferred_element_type=jnp.float32)
    sorted_rows = sorted_rows + jnp.dot(low, order, preferred_element_type=jnp.float32)
    own = sorted_rows[: 2 * CHANNELS] + past
    later = sorted_rows[2 * CHANNELS :]
    quads = [own[:CHANNELS], own[CHANNELS:], later[:CHANNELS], later[CHANNELS:]]
    lane = lane[:CHANNELS]
    for kind in range(4):
        value = quads[kind] * factor
        power = value * value
        power = power * power
        power = power * power
        power = power * power
        value = jnp.where(value < 0.0, -power, power)
        if kind >= 2:
            value = jnp.where(lane < (TAPS - 1) * IN_BLK, value, shift)
        value = pltpu.roll(value, (lax.axis_index("zl") % 2 * 2 + lax.axis_index("c")) * IN_BLK, 1)
        for copy in range(2):
            rows_ref[pl.ds(4 * copy + kind, CHANNELS, 8), :] = value
    out_ref[...] = rows_ref[...].astype(jnp.bfloat16)


def decode_kernel(got_ref, sums_ref, passed_ref):
    lane_group = lax.broadcasted_iota(jnp.int32, (8, LANES), 1) // IN_BLK
    row = lax.broadcasted_iota(jnp.int32, (8, LANES), 0)
    upper = row % 4 >= 2
    for tile in range(8):
        quarters = [got_ref[pl.ds((4 * tile + g) * 8, 8), :].astype(jnp.float32) for g in range(4)]
        halves = [jnp.where(lane_group < 2, quarters[-slot % 4], quarters[(2 - slot) % 4]) for slot in range(4)]
        codes = [jnp.where(lane_group % 2 == 0, halves[slot], halves[slot - 1]) for slot in range(4)]
        codes = [pltpu.roll(code, (-slot % 4) * IN_BLK, 1) if slot else code for slot, code in enumerate(codes)]
        shift = jnp.where(upper, codes[3], pltpu.roll(codes[3], 6, 0))
        values = []
        moved = []
        for code in codes:
            size = jnp.maximum(jnp.abs(code), 2.0**-126)
            values.append(code * jnp.exp2(jnp.log2(size) * (1.0 / POWER - 1.0) + shift))
        for slot in range(TAPS - 1):
            moved.append(pltpu.roll(values[slot], 2, 0))
            values[slot] = values[slot] + jnp.where(row >= 4, moved[slot], 0.0)
        for pair in range(2):
            rows = pl.ds(8 * pair, 8)
            sums_ref[tile, rows, :] = jnp.where(upper, pltpu.roll(values[2 * pair + 1], 2, 0), values[2 * pair])
        second = jnp.where(row < 4, pltpu.roll(moved[1], 2, 0), 0.0)
        passed_ref[tile, :8, :] = jnp.where(row < 2, moved[0], second)
        passed_ref[tile, 8:, :] = jnp.where(row < 2, moved[2], 0.0)


def gram_kernel(*refs):
    sums_refs, passed_refs, out_hbm, vis_ref, sems = refs[:4], refs[4:8], *refs[8:]

    def frames_of(tile):
        return jnp.concatenate([sums_refs[i][tile] + passed_refs[i - 1][tile] for i in range(4)], axis=0)

    tile = 2 * lax.axis_index("y") + lax.axis_index("zh")
    left = frames_of(tile) * (1.0 / (FRQ * FR_BLK))
    real = lax.broadcasted_iota(jnp.int32, left.shape, 0) % 2 == 0
    turned = jnp.where(real, pltpu.roll(left, left.shape[0] - 1, 0), -pltpu.roll(left, 1, 0))
    high, low = two_terms(jnp.concatenate([left, turned], axis=1))
    left = jnp.concatenate([high, high, low], axis=0)
    row = lax.broadcasted_iota(jnp.int32, (2 * LANES, 2 * LANES), 0)
    col = lax.broadcasted_iota(jnp.int32, (2 * LANES, 2 * LANES), 1)
    order = jnp.where(col == row % 2 * LANES + row // 2, 1.0, 0.0).astype(jnp.bfloat16)
    left = lax.dot_general(order, left, (((1,), (1,)), ((), ())), preferred_element_type=jnp.float32)
    left = left.astype(jnp.bfloat16)
    copies = []
    for pair in range(4):
        high, low = two_terms(jnp.concatenate([frames_of(2 * pair + i) for i in range(2)], axis=1))
        right = jnp.concatenate([high, low, high], axis=0)
        vis = jnp.dot(left, right, preferred_element_type=jnp.float32)
        for i in range(2):
            tile = 2 * pair + i
            vis_ref.at[tile].reshape(2 * LANES, LANES)[...] = vis[:, i * LANES : (i + 1) * LANES]
            copies.append(pltpu.make_async_copy(vis_ref.at[tile], out_hbm.at[:, tile], sems.at[tile]))
            copies[-1].start()
    for copy in copies:
        copy.wait()


def body(voltages, history, window):
    vmem = pl.BlockSpec(memory_space=pltpu.VMEM)
    hbm = pl.BlockSpec(memory_space=pl.ANY)
    past = history.transpose(1, 0, 2).reshape((TAPS - 1) * IN_BLK, SAMPLES)
    chunks = pl.pallas_call(
        transform_kernel,
        out_shape=pltpu.VMEM((2 * LANES, LANES), jnp.bfloat16),
        in_specs=[hbm] * 4,
        out_specs=vmem,
        scratch_shapes=[
            pltpu.VMEM((SAMPLES // LANES, IN_BLK, FR_BLK, LANES), jnp.bfloat16),
            pltpu.VMEM(past.shape, jnp.bfloat16),
            pltpu.VMEM(window.shape, jnp.float32),
            pltpu.VMEM((4 * CHANNELS, LANES), jnp.float32),
            pltpu.VMEM((2 * LANES, LANES), jnp.float32),
            pltpu.VMEM((2 * CHANNELS, LANES), jnp.float32),
            pltpu.SemaphoreType.DMA((4,)),
        ],
        name="transform",
    )(voltages, past, window, jnp.asarray(dft_start()))
    chunks = chunks.reshape(2 * CHANNELS, 4, LANES)
    mine = lax.all_to_all(chunks, ("x", "zl", "c", "zh"), 0, 0, tiled=True).reshape(2 * LANES, LANES)
    ahead, behind, across = (lax.ppermute(mine, "y", [(i, (i + k) % 4) for i in range(4)]) for k in (1, 3, 2))
    sums, passed = [], []
    for i, piece in enumerate((behind, across, ahead, mine)):
        found = pl.pallas_call(
            decode_kernel,
            out_shape=[pltpu.VMEM((8, 2 * 8, LANES), jnp.float32)] * 2,
            in_specs=[vmem],
            out_specs=[vmem] * 2,
            name=f"decode{i}",
        )(pltpu.with_memory_space_constraint(piece, pltpu.VMEM))
        sums.append(pltpu.with_memory_space_constraint(found[0], pltpu.VMEM))
        passed.append(pltpu.with_memory_space_constraint(found[1], pltpu.VMEM))
    tiles = pl.pallas_call(
        gram_kernel,
        out_shape=jax.ShapeDtypeStruct((LANES, 8, 2, LANES), jnp.float32),
        in_specs=[vmem] * 8,
        out_specs=hbm,
        scratch_shapes=[pltpu.VMEM((8, LANES, 2, LANES), jnp.float32), pltpu.SemaphoreType.DMA((8,))],
        name="gram",
    )(*sums, *passed)
    return tiles.transpose(0, 2, 1, 3).reshape(LANES, 1, 2, 8 * LANES)


def solution(mesh):
    fine = jax.sharding.Mesh(mesh.devices.reshape(4, 4, 2, 4, 2), ("x", "zl", "c", "y", "zh"))
    inp, frq = ("x", "zl", "c"), ("y", "zh")
    return jax.shard_map(
        body,
        mesh=fine,
        in_specs=(P(inp, frq, None), P(inp, None, None), P()),
        out_specs=P(frq, inp, None, None),
        check_vma=False,
    )
```

```python
import math

import jax
import jax.numpy as jnp
import numpy as np
from jax import lax
from jax.experimental import pallas as pl
from jax.experimental.pallas import tpu as pltpu
from jax.sharding import PartitionSpec as P

TAPS = 4
SAMPLES = 2048
CHANNELS = 32
CHAN_FIRST = 496
IN_BLK = 32
FR_BLK = 4
FRQ = 8
LANES = 128
STEP = 256
POWER = 16
TOP = 7


def dft_start():
    bins = np.arange(CHANNELS, dtype=np.int64) + CHAN_FIRST
    turns = bins[:, None] * np.arange(LANES, dtype=np.int64)[None, :] % SAMPLES
    begin = np.exp(turns * (-2j * math.pi / SAMPLES)) / math.sqrt(SAMPLES)
    turn = np.exp(bins[:, None] * LANES % SAMPLES * (-2j * math.pi / SAMPLES)) * np.ones((1, LANES))
    return np.concatenate([begin.real, begin.imag, turn.real, turn.imag]).astype(np.float32)


def two_terms(x):
    high = x.astype(jnp.bfloat16)
    low = (x - high.astype(jnp.float32)).astype(jnp.bfloat16)
    return high, low


def products(start_ref, window_ref, taps, frames_at):
    dims = (((1,), (1,)), ((), ()))
    total = None
    real, imag, turn_real, turn_imag = (start_ref[part * CHANNELS : (part + 1) * CHANNELS, :] for part in range(4))
    for step in range(SAMPLES // STEP):
        cols = slice(step * STEP, (step + 1) * STEP)
        table = []
        for _ in range(STEP // LANES):
            table.append(jnp.concatenate([real, imag], axis=0))
            real, imag = real * turn_real - imag * turn_imag, real * turn_imag + imag * turn_real
        table = jnp.concatenate(table, axis=1)
        weights = jnp.concatenate([table * window_ref[tap : tap + 1, cols] for tap in range(taps)], axis=0)
        high, low = two_terms(weights)
        frames = frames_at(step)
        part = lax.dot_general(jnp.concatenate([high, low], axis=0), frames, dims, preferred_element_type=jnp.float32)
        total = part if total is None else total + part
    total = total[: total.shape[0] // 2] + total[total.shape[0] // 2 :]
    return [total[tap * 2 * CHANNELS : (tap + 1) * 2 * CHANNELS] for tap in range(taps)]


def transform_kernel(volt_hbm, hist_hbm, window_hbm, start_hbm, out_ref,
                     volt_ref, hist_ref, window_ref, start_ref, rows_ref, past_ref, sems):
    first = (lax.axis_index("y") == 0) & (lax.axis_index("zh") == 0)
    hist_copy = pltpu.make_async_copy(hist_hbm, hist_ref, sems.at[3])
    pltpu.make_async_copy(window_hbm, window_ref, sems.at[0]).start()
    pltpu.make_async_copy(start_hbm, start_ref, sems.at[1]).start()
    for tile in range(SAMPLES // LANES):
        pltpu.make_async_copy(volt_hbm.at[:, :, pl.ds(tile * LANES, LANES)], volt_ref.at[tile], sems.at[2]).start()

    @pl.when(first)
    def _():
        hist_copy.start()

    lane = lax.broadcasted_iota(jnp.int32, (2 * CHANNELS, LANES), 1)
    past_ref[...] = jnp.zeros((2 * CHANNELS, LANES), jnp.float32)
    pltpu.make_async_copy(window_hbm, window_ref, sems.at[0]).wait()
    pltpu.make_async_copy(start_hbm, start_ref, sems.at[1]).wait()

    @pl.when(first)
    def _():
        hist_copy.wait()

        def frames_at(step):
            rows = hist_ref[:, step * STEP : (step + 1) * STEP]
            return jnp.concatenate([rows, jnp.zeros((IN_BLK, STEP), jnp.bfloat16)], axis=0)

        past = jnp.zeros((2 * CHANNELS, LANES), jnp.float32)
        for tap, before in enumerate(products(start_ref, window_ref, TAPS - 1, frames_at)):
            if tap:
                before = pltpu.roll(before, LANES - tap * IN_BLK, 1)
            past = past + jnp.where(lane < (TAPS - 1 - tap) * IN_BLK, before, 0.0)
        past_ref[...] = past

    pltpu.make_async_copy(volt_ref, volt_ref, sems.at[2]).wait()

    def frames_at(step):
        tiles = range(step * STEP // LANES, (step + 1) * STEP // LANES)
        return jnp.concatenate([volt_ref.at[tile].reshape(LANES, LANES)[...] for tile in tiles], axis=1)

    frame = lane % FR_BLK
    own = later = None
    for tap, here in enumerate(products(start_ref, window_ref, TAPS, frames_at)):
        moved = TAPS - 1 - tap
        if moved == 0:
            own = own + here
            continue
        kept = jnp.where(frame < moved, 0.0, pltpu.roll(here, moved, 1))
        passed = jnp.where(frame < moved, pltpu.roll(here, LANES - FR_BLK + moved, 1), 0.0)
        own = kept if own is None else own + kept
        later = passed if later is None else later + passed
    last = (lax.axis_index("y") == 3) & (lax.axis_index("zh") == 1)
    later = jnp.where(last, 0.0, later)
    past = past_ref[...]
    top = jnp.maximum(jnp.maximum(jnp.abs(own), jnp.abs(later)), jnp.abs(past))
    top = jnp.maximum(top[:CHANNELS], top[CHANNELS:])
    top = jnp.maximum(jnp.max(top, axis=1, keepdims=True), 2.0**-100)
    shift = jnp.broadcast_to(jnp.ceil(jnp.log2(top)) - (TOP - 1), (CHANNELS, LANES))
    factor = jnp.exp2(-shift)
    row = lax.broadcasted_iota(jnp.int32, (LANES, LANES), 0)
    col = lax.broadcasted_iota(jnp.int32, (LANES, LANES), 1)
    order = jnp.where(col == row % FR_BLK * IN_BLK + row // FR_BLK, 1.0, 0.0).astype(jnp.bfloat16)
    high, low = two_terms(jnp.concatenate([own, later], axis=0))
    sorted_rows = jnp.dot(high, order, preferred_element_type=jnp.float32)
    sorted_rows = sorted_rows + jnp.dot(low, order, preferred_element_type=jnp.float32)
    own = sorted_rows[: 2 * CHANNELS] + past
    later = sorted_rows[2 * CHANNELS :]
    quads = [own[:CHANNELS], own[CHANNELS:], later[:CHANNELS], later[CHANNELS:]]
    lane = lane[:CHANNELS]
    for kind in range(4):
        value = quads[kind] * factor
        power = value * value
        power = power * power
        power = power * power
        power = power * power
        value = jnp.where(value < 0.0, -power, power)
        if kind >= 2:
            value = jnp.where(lane < (TAPS - 1) * IN_BLK, value, shift)
        value = pltpu.roll(value, (lax.axis_index("zl") % 2 * 2 + lax.axis_index("c")) * IN_BLK, 1)
        for copy in range(2):
            rows_ref[pl.ds(4 * copy + kind, CHANNELS, 8), :] = value
    out_ref[...] = rows_ref[...].astype(jnp.bfloat16)


def decode_kernel(got_ref, sums_ref, passed_ref, *order_ref):
    lane_group = lax.broadcasted_iota(jnp.int32, (8, LANES), 1) // IN_BLK
    row = lax.broadcasted_iota(jnp.int32, (8, LANES), 0)
    upper = row % 4 >= 2
    for tile in range(8):
        quarters = [got_ref[pl.ds((4 * tile + g) * 8, 8), :].astype(jnp.float32) for g in range(4)]
        halves = [jnp.where(lane_group < 2, quarters[-slot % 4], quarters[(2 - slot) % 4]) for slot in range(4)]
        codes = [jnp.where(lane_group % 2 == 0, halves[slot], halves[slot - 1]) for slot in range(4)]
        codes = [pltpu.roll(code, (-slot % 4) * IN_BLK, 1) if slot else code for slot, code in enumerate(codes)]
        shift = jnp.where(upper, codes[3], pltpu.roll(codes[3], 6, 0))
        values = []
        moved = []
        for code in codes:
            size = jnp.maximum(jnp.abs(code), 2.0**-126)
            values.append(code * jnp.exp2(jnp.log2(size) * (1.0 / POWER - 1.0) + shift))
        for slot in range(TAPS - 1):
            moved.append(pltpu.roll(values[slot], 2, 0))
            values[slot] = values[slot] + jnp.where(row >= 4, moved[slot], 0.0)
        for pair in range(2):
            rows = pl.ds(8 * pair, 8)
            sums_ref[tile, rows, :] = jnp.where(upper, pltpu.roll(values[2 * pair + 1], 2, 0), values[2 * pair])
        second = jnp.where(row < 4, pltpu.roll(moved[1], 2, 0), 0.0)
        passed_ref[tile, :8, :] = jnp.where(row < 2, moved[0], second)
        passed_ref[tile, 8:, :] = jnp.where(row < 2, moved[2], 0.0)
    if order_ref:
        row = lax.broadcasted_iota(jnp.int32, (2 * LANES, 2 * LANES), 0)
        col = lax.broadcasted_iota(jnp.int32, (2 * LANES, 2 * LANES), 1)
        order = jnp.where(col == row % 2 * LANES + row // 2, 1.0, 0.0)
        order_ref[0][...] = order.astype(jnp.bfloat16)


def gram_kernel(*refs):
    sums_refs, passed_refs, order_ref, out_hbm, vis_ref, sems = refs[:4], refs[4:8], *refs[8:]

    def frames_of(tile):
        return jnp.concatenate([sums_refs[i][tile] + passed_refs[i - 1][tile] for i in range(4)], axis=0)

    tile = 2 * lax.axis_index("y") + lax.axis_index("zh")
    left = frames_of(tile) * (1.0 / (FRQ * FR_BLK))
    real = lax.broadcasted_iota(jnp.int32, left.shape, 0) % 2 == 0
    turned = jnp.where(real, pltpu.roll(left, left.shape[0] - 1, 0), -pltpu.roll(left, 1, 0))
    high, low = two_terms(jnp.concatenate([left, turned], axis=1))
    left = jnp.concatenate([high, high, low], axis=0)
    left = lax.dot_general(order_ref[...], left, (((1,), (1,)), ((), ())), preferred_element_type=jnp.float32)
    left = left.astype(jnp.bfloat16)
    copies = []
    for pair in range(4):
        high, low = two_terms(jnp.concatenate([frames_of(2 * pair + i) for i in range(2)], axis=1))
        right = jnp.concatenate([high, low, high], axis=0)
        vis = jnp.dot(left, right, preferred_element_type=jnp.float32)
        for i in range(2):
            tile = 2 * pair + i
            vis_ref.at[tile].reshape(2 * LANES, LANES)[...] = vis[:, i * LANES : (i + 1) * LANES]
            copies.append(pltpu.make_async_copy(vis_ref.at[tile], out_hbm.at[:, tile], sems.at[tile]))
            copies[-1].start()
    for copy in copies:
        copy.wait()


def body(voltages, history, window):
    vmem = pl.BlockSpec(memory_space=pltpu.VMEM)
    hbm = pl.BlockSpec(memory_space=pl.ANY)
    past = history.transpose(1, 0, 2).reshape((TAPS - 1) * IN_BLK, SAMPLES)
    chunks = pl.pallas_call(
        transform_kernel,
        out_shape=pltpu.VMEM((2 * LANES, LANES), jnp.bfloat16),
        in_specs=[hbm] * 4,
        out_specs=vmem,
        scratch_shapes=[
            pltpu.VMEM((SAMPLES // LANES, IN_BLK, FR_BLK, LANES), jnp.bfloat16),
            pltpu.VMEM(past.shape, jnp.bfloat16),
            pltpu.VMEM(window.shape, jnp.float32),
            pltpu.VMEM((4 * CHANNELS, LANES), jnp.float32),
            pltpu.VMEM((2 * LANES, LANES), jnp.float32),
            pltpu.VMEM((2 * CHANNELS, LANES), jnp.float32),
            pltpu.SemaphoreType.DMA((4,)),
        ],
        name="transform",
    )(voltages, past, window, jnp.asarray(dft_start()))
    chunks = chunks.reshape(2 * CHANNELS, 4, LANES)
    mine = lax.all_to_all(chunks, ("x", "zl", "c", "zh"), 0, 0, tiled=True).reshape(2 * LANES, LANES)
    ahead, behind, across = (lax.ppermute(mine, "y", [(i, (i + k) % 4) for i in range(4)]) for k in (1, 3, 2))
    sums, passed = [], []
    for i, piece in enumerate((behind, across, ahead, mine)):
        extra = [pltpu.VMEM((2 * LANES, 2 * LANES), jnp.bfloat16)] if i == 3 else []
        found = pl.pallas_call(
            decode_kernel,
            out_shape=[pltpu.VMEM((8, 2 * 8, LANES), jnp.float32)] * 2 + extra,
            in_specs=[vmem],
            out_specs=[vmem] * (2 + len(extra)),
            name=f"decode{i}",
        )(pltpu.with_memory_space_constraint(piece, pltpu.VMEM))
        sums.append(pltpu.with_memory_space_constraint(found[0], pltpu.VMEM))
        passed.append(pltpu.with_memory_space_constraint(found[1], pltpu.VMEM))
    tiles = pl.pallas_call(
        gram_kernel,
        out_shape=jax.ShapeDtypeStruct((LANES, 8, 2, LANES), jnp.float32),
        in_specs=[vmem] * 9,
        out_specs=hbm,
        scratch_shapes=[pltpu.VMEM((8, LANES, 2, LANES), jnp.float32), pltpu.SemaphoreType.DMA((8,))],
        name="gram",
    )(*sums, *passed, pltpu.with_memory_space_constraint(found[2], pltpu.VMEM))
    return tiles.transpose(0, 2, 1, 3).reshape(LANES, 1, 2, 8 * LANES)


def solution(mesh):
    fine = jax.sharding.Mesh(mesh.devices.reshape(4, 4, 2, 4, 2), ("x", "zl", "c", "y", "zh"))
    inp, frq = ("x", "zl", "c"), ("y", "zh")
    return jax.shard_map(
        body,
        mesh=fine,
        in_specs=(P(inp, frq, None), P(inp, None, None), P()),
        out_specs=P(frq, inp, None, None),
        check_vma=False,
    )
```
